32 devices in a mesh: groups: 2 (over x), tm: 8 (over z, y), band: 2 (over core).
Axes of the slice: x: 2, y: 2, z: 4, core: 2. Of those that a mesh axis runs over, the one named last changes fastest.
Arguments:
- series: float32 [262144], P(('groups', 'tm')), parts along dimension 0, may hold values from -40 to 40
- tail: float32 [512], P('groups'), parts along dimension 0, may hold values from -6 to 6
- band_starts: int32 [4], P('groups'), parts along dimension 0, may hold values from 0 to 3968, as said below
Outputs:
- row_profile: float32 [262144], P(('groups', 'tm')), parts along dimension 0
- col_profile: float32 [262144], P(('groups', 'tm')), parts along dimension 0
The draws below stay inside these ranges and needn't reach their ends.
There are 2 independent parts, one for each index of `groups`. The reference program is written for one: setup_inputs(seed, part) draws one part's arguments, and reference() takes and returns one part's arrays. A program takes and returns all parts, laid end to end along the dimension named above; each array names one. Nothing has to cross between parts.
Inputs may be any that keep to these rules, and one draw needn't show every extreme that they name: `band_starts`: one entry equals 3968.
All inputs are finite; a program needn't handle non-finite values.
Results may differ from the reference program's by a relative error of at most 0.00061.
Values sent between devices are 32-bit elements; how exact they have to be, the bound alone decides.
No kernel may reach another device: no remote copies, remote signals or barrier semaphores. Data moves between devices by JAX's collectives and lax.ppermute only.
A program may use at most 64 MiB of HBM per device.

```python
import jax
import jax.numpy as jnp
from jax import lax

M = 256
TILE = 128
OFF_DEV = 128
BAND_SPAN = 4096
SAMPLES = 131072
BAND_BASE = 65536
N_BAND = 2


def draw_series(key, part):
    key_offset, key_scale, key_noise = jax.random.split(jax.random.fold_in(key, 11), 3)
    blocks = SAMPLES // 128
    offset = jax.random.uniform(key_offset, (blocks,), jnp.float32, -2.0, 2.0)
    scales = jnp.exp(jax.random.uniform(key_scale, (blocks,), jnp.float32, -0.69, 0.69))
    noise = jnp.clip(jax.random.normal(key_noise, (blocks, 128), jnp.float32), -6.0, 6.0)
    return (offset[:, None] + scales[:, None] * noise).reshape(SAMPLES)


def draw_band_starts(key, part):
    key_values, key_pick = jax.random.split(jax.random.fold_in(key, 23))
    highest = BAND_SPAN - OFF_DEV
    values = jax.random.randint(key_values, (N_BAND,), 0, highest + 1)
    chosen = jax.random.randint(key_pick, (), 0, N_BAND)
    return jnp.where(jnp.arange(N_BAND) == chosen, highest, values).astype(jnp.int32)


def centred(stream_key, dims, scale, reach, kind=jnp.bfloat16):
    return jnp.clip(scale * jax.random.normal(stream_key, dims, jnp.float32), -reach, reach).astype(kind)


def setup_inputs(seed: int = 0, part: int = 0) -> dict:
    key_list = jax.random.split(jax.random.key(seed), 4)
    own_keys = jax.random.split(jax.random.fold_in(key_list[3], part), 4)
    return {
        "series": draw_series(jax.random.fold_in(jax.random.fold_in(key_list[3], part), 71), part),
        "tail": centred(own_keys[1], (M,), 1.0, 6.0, jnp.float32),
        "band_starts": draw_band_starts(jax.random.fold_in(jax.random.fold_in(key_list[3], part), 71), part),
    }


EPS = 1e-06
tile_batch = 16

def hankel(samples, tile_count):
    length = tile_count * TILE + M
    shifted = jnp.stack([lax.slice_in_dim(samples, offset, offset + length) for offset in range(TILE)])
    blocks = shifted.reshape(TILE, length // TILE, TILE)
    joined = jnp.concatenate([blocks[:, stride:stride + tile_count] for stride in range(M // TILE)], axis=2)
    return jnp.swapaxes(joined, 0, 1)

def moments(matrix):
    center = lax.optimization_barrier(jnp.mean(matrix, axis=-1))
    spread = matrix - center[..., None]
    factor = lax.rsqrt(lax.optimization_barrier(jnp.sum(spread * spread, axis=-1)) + M * EPS)
    return (center, factor)

def normed(matrix, center, factor):
    return ((matrix - center[..., None]) * factor[..., None]).astype(jnp.bfloat16)

def score_group(row_z, col_z, room_left):
    tile_count = row_z.shape[0]
    row_wide = row_z.astype(jnp.float32)
    near_scores = jnp.einsum('tim,tjm->tij', row_wide, col_z[:-1].astype(jnp.float32), precision=lax.Precision.HIGHEST)
    far_scores = jnp.einsum('tim,tjm->tij', row_wide, col_z[1:, :OFF_DEV].astype(jnp.float32), precision=lax.Precision.HIGHEST)
    row_near = lax.broadcasted_iota(jnp.int32, (TILE, TILE), 0)
    col_near = lax.broadcasted_iota(jnp.int32, (TILE, TILE), 1)
    row_far = lax.broadcasted_iota(jnp.int32, (TILE, OFF_DEV), 0)
    col_far = lax.broadcasted_iota(jnp.int32, (TILE, OFF_DEV), 1)
    tile_index = jnp.arange(tile_count, dtype=jnp.int32)[:, None, None]
    keep_near = (col_near >= row_near)[None] & (col_near - row_near < OFF_DEV)[None] & (tile_index * TILE + col_near[None] < room_left)
    keep_far = (TILE + col_far - row_far < OFF_DEV)[None] & ((tile_index + 1) * TILE + col_far[None] < room_left)
    near_scores = jnp.where(keep_near, near_scores, -1.0)
    far_scores = jnp.where(keep_far, far_scores, -1.0)
    best_rows = jnp.maximum(near_scores.max(axis=2), far_scores.max(axis=2)).reshape(-1)
    floor_row = jnp.full((1, TILE), -1.0, near_scores.dtype)
    upper_part = jnp.concatenate([near_scores.max(axis=1), floor_row], axis=0)
    far_cols = jnp.pad(far_scores.max(axis=1), ((0, 0), (0, TILE - OFF_DEV)), constant_values=-1.0)
    lower_part = jnp.concatenate([floor_row, far_cols], axis=0)
    return (best_rows, jnp.maximum(upper_part, lower_part).reshape(-1))

def reference(series, tail, band_starts):
    length = series.shape[0]
    group_rows = tile_batch * TILE
    group_count = length // group_rows
    spare_cells = BAND_BASE + BAND_SPAN + 2 * group_rows + M + 2 * TILE
    extended = jnp.concatenate([series, tail, jnp.zeros((spare_cells,), series.dtype)])
    initial = jnp.full((length + spare_cells,), -1.0, series.dtype)

    def advance(columns, group_index):
        first_row = group_index * group_rows
        row_piece = lax.dynamic_slice_in_dim(extended, first_row, group_rows + M + TILE)
        matrix = hankel(row_piece, tile_batch)
        center, factor = moments(matrix)
        row_z = normed(matrix, center, factor)
        row_best = None
        for band_index in range(N_BAND):
            col_begin = (first_row + BAND_BASE + band_starts[band_index]).astype(jnp.int32)
            col_piece = lax.dynamic_slice_in_dim(extended, col_begin, (tile_batch + 2) * TILE + M)
            col_matrix = hankel(col_piece, tile_batch + 1)
            col_center, col_factor = moments(col_matrix)
            col_z = normed(col_matrix, col_center, col_factor)
            row_found, col_reach = score_group(row_z, col_z, length - col_begin)
            current = lax.dynamic_slice_in_dim(columns, col_begin, (tile_batch + 1) * TILE)
            columns = lax.dynamic_update_slice(columns, jnp.maximum(current, col_reach), (col_begin,))
            row_best = row_found if row_best is None else jnp.maximum(row_best, row_found)
        return (columns, row_best)
    columns, row_found = lax.scan(advance, initial, jnp.arange(group_count, dtype=jnp.int32))
    return (row_found.reshape(length), columns[:length])
```

```python
import functools

import jax
import jax.numpy as jnp
from jax import lax
from jax.experimental import pallas as pl
from jax.experimental.pallas import tpu as pltpu
from jax.sharding import PartitionSpec as P

M = 256
LANES = 128
OFF_DEV = 128
BAND_SPAN = 4096
BAND_BASE = 65536
EPS = 1e-06

WIN = M // LANES
BEFORE = BAND_SPAN // LANES + 1
AFTER = BEFORE + WIN


def window_moments(samples):
    count = samples.shape[0]
    lane = lax.broadcasted_iota(jnp.int32, samples.shape, 1)

    def ahead(values, distance):
        below = pltpu.roll(values, count - 1, 0)
        if distance == LANES:
            return below
        joined = jnp.where(lane < distance, below, values)
        return pltpu.roll(joined, LANES - distance, 1)

    center = samples
    spread = None
    size = 1
    while size < M:
        later = ahead(center, size)
        gap = later - center
        step = gap * gap * (0.5 * size)
        spread = step if spread is None else spread + ahead(spread, size) + step
        center = 0.5 * (later + center)
        size *= 2
    return center, spread


def profile_kernel(
    geometry,
    starts_ref,
    own_ref,
    halo_ref,
    tail_ref,
    main_ref,
    side_ref,
    last_ref,
    out_ref,
    own_s,
    pair_s,
    shifted,
    center_s,
    factor_s,
    near_s,
):
    devices, distance, rows, tiles, role = geometry
    bands = starts_ref.shape[0]
    position = lax.axis_index("tm")
    first_row = lax.axis_index("band") * tiles if tiles < rows else 0
    is_col = position >= distance if role is None else role
    block = rows * LANES

    own_s[pl.ds(0, rows), :] = own_ref[...]
    own_s[pl.ds(rows, WIN), :] = jnp.where(position == devices - 1, tail_ref[...], halo_ref[...])
    pair_s[pl.ds(rows + AFTER, pair_s.shape[0] - rows - AFTER), :] = jnp.zeros(
        (pair_s.shape[0] - rows - AFTER, LANES), jnp.float32
    )

    @pl.when(jnp.logical_not(is_col))
    def _():
        pair_s[pl.ds(0, rows), :] = main_ref[...]
        pair_s[pl.ds(rows, AFTER), :] = side_ref[...]

        @pl.when(position == devices - distance - 1)
        def _():
            pair_s[pl.ds(rows, WIN), :] = tail_ref[...]

    @pl.when(is_col)
    def _():
        pair_s[pl.ds(0, BEFORE), :] = side_ref[pl.ds(WIN, BEFORE), :]
        pair_s[pl.ds(BEFORE, rows), :] = main_ref[...]
        pair_s[pl.ds(BEFORE + rows, WIN), :] = last_ref[...]

    lane = lax.broadcasted_iota(jnp.int32, (1, LANES), 1)
    reach = tiles + 1 + WIN
    begins = []
    for band in range(bands):
        start = starts_ref[band]
        begin = jnp.where(is_col, BEFORE * LANES - (OFF_DEV - 1) - start, start) + first_row * LANES
        begins.append(begin)
        whole, part = begin // LANES, begin % LANES
        piece = pair_s[pl.ds(whole, reach + 1), :]
        turned = pltpu.roll(piece, LANES - part, 1)
        shifted[band, pl.ds(0, reach), :] = jnp.where(lane < LANES - part, turned[:-1], turned[1:])
    shifted[bands, pl.ds(0, reach - 1), :] = own_s[pl.ds(first_row, reach - 1), :]
    center, spread = window_moments(shifted[...].reshape(-1, LANES))
    center_s[...] = center.reshape(center_s.shape)
    factor_s[...] = lax.rsqrt(spread + M * EPS).reshape(factor_s.shape)

    row_id = lax.broadcasted_iota(jnp.int32, (LANES, LANES), 0)
    col_id = lax.broadcasted_iota(jnp.int32, (LANES, LANES), 1)
    source = (row_id + col_id) % LANES
    straight = row_id + col_id < LANES
    upper = row_id >= col_id

    def turned_row(stream, row):
        line = jnp.broadcast_to(shifted[stream, pl.ds(row, 1), :], (LANES, LANES))
        return jnp.take_along_axis(line, source, axis=1)

    def hankel(stream, row):
        a, b, c = (turned_row(stream, row + s) for s in range(WIN + 1))
        return jnp.where(straight, a, b), jnp.where(straight, b, c)

    def column_form(values, tile):
        line = jnp.broadcast_to(values[pl.ds(tile, 1), :], (LANES, LANES))
        return jnp.transpose(line)

    def own_z(tile):
        low, high = hankel(bands, tile)
        center = center_s[bands, pl.ds(tile, 1), :]
        factor = factor_s[bands, pl.ds(tile, 1), :]
        return jnp.concatenate(
            [((low - center) * factor).astype(jnp.bfloat16), ((high - center) * factor).astype(jnp.bfloat16)],
            axis=0,
        )

    def pair_z(band, tile):
        low, high = hankel(band, tile)
        center = column_form(center_s.at[band], tile)
        factor = column_form(factor_s.at[band], tile)
        return jnp.concatenate(
            [((low - center) * factor).astype(jnp.bfloat16), ((high - center) * factor).astype(jnp.bfloat16)],
            axis=1,
        )

    low_edge = BEFORE * LANES - (position - distance) * block
    high_edge = (devices - position - distance) * block
    lo = jnp.where(is_col, low_edge, 0)
    hi = jnp.where(is_col, 1 << 30, high_edge)

    def step(masked, tile, before):
        here = own_z(jnp.minimum(tile, tiles - 1))
        both = jnp.concatenate([before, here], axis=1)
        far = near = None
        for band in range(bands):
            z = pair_z(band, tile)
            scores = jnp.dot(z, both, preferred_element_type=jnp.float32)
            if masked:
                index = begins[band] + tile * LANES + lax.broadcasted_iota(jnp.int32, (LANES, 1), 0)
                scores = jnp.where((index >= lo) & (index < hi), scores, -1.0)
            far = scores[:, :LANES] if far is None else jnp.maximum(far, scores[:, :LANES])
            near = scores[:, LANES:] if near is None else jnp.maximum(near, scores[:, LANES:])
        best = jnp.where(upper, near_s[...], far)
        best = jnp.maximum(jnp.max(best, axis=0, keepdims=True), -1.0)
        near_s[...] = near

        @pl.when(tile > 0)
        def _():
            out_ref[pl.ds(tile - 1, 1), :] = best

        return here

    first_full, last_full = jnp.int32(0), jnp.int32(tiles + 1)
    for begin in begins:
        first_full = jnp.maximum(first_full, (lo - begin + LANES - 1) // LANES)
        last_full = jnp.minimum(last_full, (hi - begin) // LANES)
    first_full = jnp.clip(first_full, 0, tiles + 1)
    last_full = jnp.clip(last_full, first_full, tiles + 1)
    before = jnp.zeros((M, LANES), jnp.bfloat16)
    before = lax.fori_loop(0, first_full, functools.partial(step, True), before)
    before = lax.fori_loop(first_full, last_full, functools.partial(step, False), before)
    lax.fori_loop(last_full, tiles + 1, functools.partial(step, True), before)


def profile(geometry, starts, own, halo, tail, main, side, last):
    devices, distance, rows, tiles, role = geometry
    bands = starts.shape[0]
    vmem = pl.BlockSpec(memory_space=pltpu.VMEM)
    pad = -(-(tiles + 2 + WIN) // 8) * 8
    return pl.pallas_call(
        functools.partial(profile_kernel, geometry),
        out_shape=jax.ShapeDtypeStruct((tiles, LANES), jnp.float32),
        in_specs=[pl.BlockSpec(memory_space=pltpu.SMEM)] + [vmem] * 6,
        out_specs=vmem,
        scratch_shapes=[
            pltpu.VMEM((rows + 8, LANES), jnp.float32),
            pltpu.VMEM((-(-(rows + AFTER + 2) // 8) * 8, LANES), jnp.float32),
            pltpu.VMEM((bands + 1, pad, LANES), jnp.float32),
            pltpu.VMEM((bands + 1, pad, LANES), jnp.float32),
            pltpu.VMEM((bands + 1, pad, LANES), jnp.float32),
            pltpu.VMEM((LANES, LANES), jnp.float32),
        ],
    )(starts, own, halo, tail, main, side, last)


def body(split, series, tail, band_starts):
    block_len = series.shape[0]
    rows = block_len // LANES
    devices = lax.axis_size("tm")
    distance = BAND_BASE // block_len
    cores = lax.axis_size("band") if split else 1
    tiles = rows // cores
    position = lax.axis_index("tm")
    own = series.reshape(rows, LANES)
    tail = tail.reshape(WIN, LANES)
    head = own[:WIN]

    def move(value, steps):
        route = [(d - s, d) for d, s in steps if 0 <= d - s < devices]
        return lax.ppermute(value, "tm", route)

    everyone = range(devices)
    halo = move(head, [(d, -1) for d in everyone])
    row_side = [d for d in everyone if d < devices - distance]
    col_side = [d for d in everyone if d >= distance]
    last = move(head, [(d, distance - 1) for d in col_side])
    if devices <= 2 * distance:
        main = move(own, [(d, -distance) for d in row_side] + [(d, distance) for d in col_side])
        begin = jnp.where(position >= distance, 0, rows - AFTER)
        piece = lax.dynamic_slice_in_dim(own, begin, AFTER)
        side = move(piece, [(d, -distance - 1) for d in row_side] + [(d, distance + 1) for d in col_side])
        found = [profile((devices, distance, rows, tiles, None), band_starts, own, halo, tail, main, side, last)]
    else:
        main = move(own, [(d, -distance) for d in row_side])
        side = move(own[:AFTER], [(d, -distance - 1) for d in row_side])
        found = [profile((devices, distance, rows, tiles, False), band_starts, own, halo, tail, main, side, last)]
        main = move(own, [(d, distance) for d in col_side])
        side = move(own[rows - AFTER :], [(d, distance + 1) for d in col_side])
        found.append(
            profile((devices, distance, rows, tiles, True), band_starts, own, halo, tail, main, side, last)
        )
    if cores > 1:
        ring = [(i, (i + 1) % cores) for i in range(cores)]
        first = lax.axis_index("band") == 0
        whole = []
        for part in found:
            other = lax.ppermute(part, "band", ring)
            whole.append(jnp.concatenate([jnp.where(first, part, other), jnp.where(first, other, part)]))
        found = whole
    is_row, is_col = position < devices - distance, position >= distance
    row_best = jnp.where(is_row, found[0], -1.0)
    col_best = jnp.where(is_col, found[-1], -1.0)
    return row_best.reshape(-1), col_best.reshape(-1)


SPLIT = True


def solution(mesh):
    placed = (P(("groups", "tm")), P("groups"), P("groups"))
    split = SPLIT and mesh.shape["band"] == 2
    return jax.shard_map(
        functools.partial(body, split),
        mesh=mesh,
        in_specs=placed,
        out_specs=(P(("groups", "tm")), P(("groups", "tm"))),
        check_vma=False,
    )
```

```python
import functools

import jax
import jax.numpy as jnp
from jax import lax
from jax.experimental import pallas as pl
from jax.experimental.pallas import tpu as pltpu
from jax.sharding import PartitionSpec as P

M = 256
LANES = 128
OFF_DEV = 128
BAND_SPAN = 4096
BAND_BASE = 65536
EPS = 1e-06

WIN = M // LANES
BEFORE = BAND_SPAN // LANES + 1
AFTER = BEFORE + WIN


def window_moments(samples, scratch):
    count = samples.shape[0]
    lane = lax.broadcasted_iota(jnp.int32, samples.shape, 1)
    slots = iter(range(scratch.shape[0]))

    def ahead(values, distance):
        slot = next(slots)
        scratch[slot, pl.ds(0, count), :] = values
        below = scratch[slot, pl.ds(1, count), :]
        if distance == LANES:
            return below
        joined = jnp.where(lane < distance, below, values)
        return pltpu.roll(joined, LANES - distance, 1)

    total = samples
    spread = None
    size = 1
    while size < M:
        later = ahead(total, size)
        gap = later - total
        step = gap * gap * (0.5 / size)
        spread = step if spread is None else spread + ahead(spread, size) + step
        total = later + total
        size *= 2
    return total * (1.0 / M), spread


STEPS = 15


def profile_kernel(
    geometry,
    starts_ref,
    own_ref,
    halo_ref,
    tail_ref,
    main_ref,
    side_ref,
    last_ref,
    out_ref,
    own_s,
    pair_s,
    shifted,
    center_s,
    factor_s,
    shift_s,
    turned_s,
    sheet_s,
    pair_z_s,
):
    devices, distance, rows, tiles, role, unroll = geometry
    bands = starts_ref.shape[0]
    position = lax.axis_index("tm")
    first_row = lax.axis_index("band") * tiles if tiles < rows else 0
    is_col = position >= distance if role is None else role
    block = rows * LANES

    own_s[pl.ds(0, rows), :] = own_ref[...]
    own_s[pl.ds(rows, WIN), :] = jnp.where(position == devices - 1, tail_ref[...], halo_ref[...])

    @pl.when(jnp.logical_not(is_col))
    def _():
        pair_s[pl.ds(0, rows), :] = main_ref[...]
        pair_s[pl.ds(rows, AFTER), :] = side_ref[...]

        @pl.when(position == devices - distance - 1)
        def _():
            pair_s[pl.ds(rows, WIN), :] = tail_ref[...]

    @pl.when(is_col)
    def _():
        pair_s[pl.ds(0, BEFORE), :] = side_ref[pl.ds(WIN, BEFORE), :]
        pair_s[pl.ds(BEFORE, rows), :] = main_ref[...]
        pair_s[pl.ds(BEFORE + rows, WIN), :] = last_ref[...]

    pair_s[pl.ds(rows + AFTER, pair_s.shape[0] - rows - AFTER), :] = jnp.zeros(
        (pair_s.shape[0] - rows - AFTER, LANES), jnp.float32
    )
    lane = lax.broadcasted_iota(jnp.int32, (1, LANES), 1)
    reach = tiles + 1 + WIN
    begins = []
    for band in range(bands):
        start = starts_ref[band]
        begin = jnp.where(is_col, BEFORE * LANES - (OFF_DEV - 1) - start, start) + first_row * LANES
        begins.append(begin)
        whole, part = begin // LANES, begin % LANES
        here = pair_s[pl.ds(whole, reach), :]
        below = pair_s[pl.ds(whole + 1, reach), :]
        shifted[band, pl.ds(0, reach), :] = pltpu.roll(jnp.where(lane < part, below, here), LANES - part, 1)
    shifted[bands, pl.ds(0, reach - 1), :] = own_s[pl.ds(first_row, reach - 1), :]
    center, spread = window_moments(shifted[...].reshape(-1, LANES), shift_s)
    center_s[...] = center.reshape(center_s.shape)
    factor_s[...] = lax.rsqrt(spread + M * EPS).reshape(factor_s.shape)

    row_id = lax.broadcasted_iota(jnp.int32, (LANES, LANES), 0)
    col_id = lax.broadcasted_iota(jnp.int32, (LANES, LANES), 1)
    ahead = col_id > row_id
    near_part = col_id >= row_id

    def turned(stream, row):
        line = jnp.broadcast_to(shifted[stream, pl.ds(row, 1), :], (LANES, LANES))
        return pltpu.roll(line, 1, 1, stride=1, stride_axis=0)

    def sheet(before, after):
        return jnp.where(ahead, after, before)

    def centered(stream, tile, low, high, scale):
        center = center_s[stream, pl.ds(tile, 1), :]
        low, high = low - center, high - center
        if scale:
            factor = factor_s[stream, pl.ds(tile, 1), :]
            low, high = low * factor, high * factor
        return jnp.concatenate([low.astype(jnp.bfloat16), high.astype(jnp.bfloat16)], axis=0)

    for stream in range(bands + 1):
        first = 1 if stream < bands else 0
        lines = [turned(stream, row) for row in range(first + 2)]
        sheets = [sheet(a, b) for a, b in zip(lines, lines[1:])]
        turned_s[stream] = lines[-1]
        sheet_s[stream] = sheets[-1]
        if stream < bands:
            pair_z_s[stream] = centered(stream, 0, sheets[0], sheets[1], True)

    low_edge = BEFORE * LANES - (position - distance) * block
    high_edge = (devices - position - distance) * block
    lo = jnp.where(is_col, low_edge, 0)
    hi = jnp.where(is_col, 1 << 30, high_edge)

    def steps(masked, group, _):
        lines = [turned_s[stream] for stream in range(bands + 1)]
        sheets = [sheet_s[stream] for stream in range(bands + 1)]
        pairs = [pair_z_s[band] for band in range(bands)]
        for inner in range(unroll):
            tile = group * unroll + inner
            following = []
            for stream in range(bands + 1):
                at = tile + 1 if stream < bands else tile
                line = turned(stream, at + 2)
                high = sheet(lines[stream], line)
                following.append(centered(stream, at, sheets[stream], high, stream < bands))
                lines[stream], sheets[stream] = line, high
            best = None
            for band in range(bands):
                both = jnp.concatenate([pairs[band], following[band]], axis=1)
                scores = lax.dot_general(
                    following[bands], both, (((0,), (0,)), ((), ())), preferred_element_type=jnp.float32
                )
                if masked:
                    index = begins[band] + tile * LANES + lax.broadcasted_iota(jnp.int32, (1, 2 * LANES), 1)
                    scores = jnp.where((index >= lo) & (index < hi), scores, -1e30)
                mixed = jnp.where(near_part, scores[:, :LANES], scores[:, LANES:])
                best = mixed if best is None else jnp.maximum(best, mixed)
                pairs[band] = following[band]
            found = jnp.max(jnp.transpose(best), axis=0, keepdims=True)
            found = found * factor_s[bands, pl.ds(tile, 1), :]
            out_ref[pl.ds(tile, 1), :] = jnp.maximum(found, -1.0)
        for stream in range(bands + 1):
            turned_s[stream] = lines[stream]
            sheet_s[stream] = sheets[stream]
        for band in range(bands):
            pair_z_s[band] = pairs[band]
        return 0

    size = unroll * LANES
    groups = tiles // unroll
    first_full, last_full = jnp.int32(0), jnp.int32(groups)
    for begin in begins:
        first_full = jnp.maximum(first_full, (lo - begin + size - 1) // size)
        last_full = jnp.minimum(last_full, (hi - begin - LANES) // size)
    first_full = jnp.clip(first_full, 0, groups)
    last_full = jnp.clip(last_full, first_full, groups)
    lax.fori_loop(0, first_full, functools.partial(steps, True), 0)
    lax.fori_loop(first_full, last_full, functools.partial(steps, False), 0)
    lax.fori_loop(last_full, groups, functools.partial(steps, True), 0)


def profile(geometry, starts, own, halo, tail, main, side, last):
    devices, distance, rows, tiles, role = geometry
    bands = starts.shape[0]
    vmem = pl.BlockSpec(memory_space=pltpu.VMEM)
    pad = -(-(tiles + 2 + WIN) // 8) * 8
    unroll = UNROLL if tiles % UNROLL == 0 else 1
    return pl.pallas_call(
        functools.partial(profile_kernel, geometry + (unroll,)),
        out_shape=jax.ShapeDtypeStruct((tiles, LANES), jnp.float32),
        in_specs=[pl.BlockSpec(memory_space=pltpu.SMEM)] + [vmem] * 6,
        out_specs=vmem,
        scratch_shapes=[
            pltpu.VMEM((rows + 8, LANES), jnp.float32),
            pltpu.VMEM((-(-(rows + AFTER + 2) // 8) * 8, LANES), jnp.float32),
            pltpu.VMEM((bands + 1, pad, LANES), jnp.float32),
            pltpu.VMEM((bands + 1, pad, LANES), jnp.float32),
            pltpu.VMEM((bands + 1, pad, LANES), jnp.float32),
            pltpu.VMEM((STEPS, (bands + 1) * pad + 8, LANES), jnp.float32),
            pltpu.VMEM((bands + 1, LANES, LANES), jnp.float32),
            pltpu.VMEM((bands + 1, LANES, LANES), jnp.float32),
            pltpu.VMEM((bands, M, LANES), jnp.bfloat16),
        ],
    )(starts, own, halo, tail, main, side, last)


def body(split, series, tail, band_starts):
    block_len = series.shape[0]
    rows = block_len // LANES
    devices = lax.axis_size("tm")
    distance = BAND_BASE // block_len
    cores = lax.axis_size("band") if split else 1
    tiles = rows // cores
    position = lax.axis_index("tm")
    own = series.reshape(rows, LANES)
    tail = tail.reshape(WIN, LANES)
    head = own[:WIN]

    def move(value, steps):
        route = [(d - s, d) for d, s in steps if 0 <= d - s < devices]
        return lax.ppermute(value, "tm", route)

    everyone = range(devices)
    halo = move(head, [(d, -1) for d in everyone])
    row_side = [d for d in everyone if d < devices - distance]
    col_side = [d for d in everyone if d >= distance]
    last = move(head, [(d, distance - 1) for d in col_side])
    if devices <= 2 * distance:
        main = move(own, [(d, -distance) for d in row_side] + [(d, distance) for d in col_side])
        begin = jnp.where(position >= distance, 0, rows - AFTER)
        piece = lax.dynamic_slice_in_dim(own, begin, AFTER)
        side = move(piece, [(d, -distance - 1) for d in row_side] + [(d, distance + 1) for d in col_side])
        found = [profile((devices, distance, rows, tiles, None), band_starts, own, halo, tail, main, side, last)]
    else:
        main = move(own, [(d, -distance) for d in row_side])
        side = move(own[:AFTER], [(d, -distance - 1) for d in row_side])
        found = [profile((devices, distance, rows, tiles, False), band_starts, own, halo, tail, main, side, last)]
        main = move(own, [(d, distance) for d in col_side])
        side = move(own[rows - AFTER :], [(d, distance + 1) for d in col_side])
        found.append(
            profile((devices, distance, rows, tiles, True), band_starts, own, halo, tail, main, side, last)
        )
    if cores > 1:
        ring = [(i, (i + 1) % cores) for i in range(cores)]
        first = lax.axis_index("band") == 0
        whole = []
        for part in found:
            other = lax.ppermute(part, "band", ring)
            whole.append(jnp.concatenate([jnp.where(first, part, other), jnp.where(first, other, part)]))
        found = whole
    is_row, is_col = position < devices - distance, position >= distance
    row_best = jnp.where(is_row, found[0], -1.0)
    col_best = jnp.where(is_col, found[-1], -1.0)
    return row_best.reshape(-1), col_best.reshape(-1)


SPLIT = True
UNROLL = 4


def solution(mesh):
    placed = (P(("groups", "tm")), P("groups"), P("groups"))
    split = SPLIT and mesh.shape["band"] == 2
    return jax.shard_map(
        functools.partial(body, split),
        mesh=mesh,
        in_specs=placed,
        out_specs=(P(("groups", "tm")), P(("groups", "tm"))),
        check_vma=False,
    )
```

```python
import functools

import jax
import jax.numpy as jnp
from jax import lax
from jax.experimental import pallas as pl
from jax.experimental.pallas import tpu as pltpu
from jax.sharding import PartitionSpec as P

M = 256
LANES = 128
OFF_DEV = 128
BAND_SPAN = 4096
BAND_BASE = 65536
EPS = 1e-06

WIN = M // LANES
BEFORE = BAND_SPAN // LANES + 1
AFTER = BEFORE + WIN


def window_moments(samples, scratch):
    count = samples.shape[0]
    lane = lax.broadcasted_iota(jnp.int32, samples.shape, 1)
    slots = iter(range(scratch.shape[0]))

    def ahead(values, distance):
        slot = next(slots)
        scratch[slot, pl.ds(0, count), :] = values
        below = scratch[slot, pl.ds(1, count), :]
        if distance == LANES:
            return below
        joined = jnp.where(lane < distance, below, values)
        return pltpu.roll(joined, LANES - distance, 1)

    total = samples
    spread = None
    size = 1
    while size < M:
        later = ahead(total, size)
        gap = later - total
        step = gap * gap * (0.5 / size)
        spread = step if spread is None else spread + ahead(spread, size) + step
        total = later + total
        size *= 2
    return total * (1.0 / M), spread


STEPS = 15


def tile_masks():
    row_id = lax.broadcasted_iota(jnp.int32, (LANES, LANES), 0)
    col_id = lax.broadcasted_iota(jnp.int32, (LANES, LANES), 1)
    return col_id > row_id, col_id >= row_id


def turned(line):
    return pltpu.roll(jnp.broadcast_to(line, (LANES, LANES)), 1, 1, stride=1, stride_axis=0)


def sheet(before, after, ahead):
    return jnp.where(ahead, after, before)


def centered(low, high, center, factor=None):
    low, high = low - center, high - center
    if factor is not None:
        low, high = low * factor, high * factor
    return jnp.concatenate([low.astype(jnp.bfloat16), high.astype(jnp.bfloat16)], axis=0)


def own_kernel(tiles, unroll, own_ref, z_ref, factor_ref, rows_s, center_s, shift_s, turned_s, sheet_s):
    first_row = lax.axis_index("band") * tiles
    count = rows_s.shape[0]
    rows_s[pl.ds(tiles, count - tiles), :] = jnp.zeros((count - tiles, LANES), jnp.float32)
    rows_s[pl.ds(0, tiles), :] = own_ref[pl.ds(first_row, tiles), :]

    @pl.when(first_row == 0)
    def _():
        rows_s[pl.ds(tiles, WIN), :] = own_ref[pl.ds(tiles, WIN), :]

    center, spread = window_moments(rows_s[...], shift_s)
    center_s[...] = center
    factor_ref[...] = lax.rsqrt(spread + M * EPS)[:tiles]
    ahead, _ = tile_masks()
    first, second = (turned(rows_s[pl.ds(row, 1), :]) for row in range(2))
    turned_s[...] = second
    sheet_s[...] = sheet(first, second, ahead)

    def group(index, _):
        line, low = turned_s[...], sheet_s[...]
        for inner in range(unroll):
            tile = index * unroll + inner
            after = turned(rows_s[pl.ds(tile + 2, 1), :])
            high = sheet(line, after, ahead)
            z_ref[tile] = jnp.transpose(centered(low, high, center_s[pl.ds(tile, 1), :]))
            line, low = after, high
        turned_s[...] = line
        sheet_s[...] = low
        return 0

    lax.fori_loop(0, tiles // unroll, group, 0)


def own_side(tiles, own):
    vmem = pl.BlockSpec(memory_space=pltpu.VMEM)
    count = -(-(tiles + WIN) // 8) * 8
    return pl.pallas_call(
        functools.partial(own_kernel, tiles, UNROLL),
        out_shape=(
            jax.ShapeDtypeStruct((tiles, LANES, M), jnp.bfloat16),
            jax.ShapeDtypeStruct((tiles, LANES), jnp.float32),
        ),
        in_specs=[vmem],
        out_specs=(vmem, vmem),
        scratch_shapes=[
            pltpu.VMEM((count, LANES), jnp.float32),
            pltpu.VMEM((count, LANES), jnp.float32),
            pltpu.VMEM((STEPS, count + 8, LANES), jnp.float32),
            pltpu.VMEM((LANES, LANES), jnp.float32),
            pltpu.VMEM((LANES, LANES), jnp.float32),
        ],
        compiler_params=pltpu.CompilerParams(vmem_limit_bytes=VMEM_LIMIT),
        cost_estimate=pl.CostEstimate(flops=20 * tiles * LANES * M, transcendentals=0, bytes_accessed=2 * tiles * LANES * M),
    )(own)


def profile_kernel(
    geometry,
    starts_ref,
    own_ref,
    halo_ref,
    tail_ref,
    main_ref,
    side_ref,
    factor_ref,
    z_ref,
    out_ref,
    late_z_s,
    late_s,
    pair_s,
    shifted,
    center_s,
    factor_s,
    shift_s,
    turned_s,
    sheet_s,
    pair_z_s,
    best_s,
):
    devices, distance, rows, tiles, role, unroll = geometry
    bands = starts_ref.shape[0]
    position = lax.axis_index("tm")
    core = lax.axis_index("band")
    is_col = position >= distance if role is None else jnp.bool_(role)
    block = rows * LANES
    groups = tiles // unroll
    early = tiles - WIN

    pair_s[pl.ds(tiles + AFTER, pair_s.shape[0] - tiles - AFTER), :] = jnp.zeros(
        (pair_s.shape[0] - tiles - AFTER, LANES), jnp.float32
    )

    @pl.when(jnp.logical_not(is_col) & (core == 0))
    def _():
        pair_s[pl.ds(0, tiles + AFTER), :] = main_ref[pl.ds(0, tiles + AFTER), :]

    @pl.when(jnp.logical_not(is_col) & (core != 0))
    def _():
        pair_s[pl.ds(0, tiles), :] = main_ref[pl.ds(rows - tiles, tiles), :]
        pair_s[pl.ds(tiles, AFTER), :] = side_ref[...]

        @pl.when(position == devices - distance - 1)
        def _():
            pair_s[pl.ds(tiles, WIN), :] = tail_ref[...]

    @pl.when(is_col & (core == 0))
    def _():
        pair_s[pl.ds(0, BEFORE), :] = side_ref[pl.ds(WIN, BEFORE), :]
        pair_s[pl.ds(BEFORE, tiles + WIN), :] = main_ref[pl.ds(0, tiles + WIN), :]

    @pl.when(is_col & (core != 0))
    def _():
        pair_s[pl.ds(0, tiles + BEFORE), :] = main_ref[pl.ds(rows - tiles - BEFORE, tiles + BEFORE), :]
        pair_s[pl.ds(tiles + BEFORE, WIN), :] = side_ref[pl.ds(0, WIN), :]

    @pl.when(core == 0)
    def _():
        late_s[pl.ds(0, 2 * WIN), :] = own_ref[pl.ds(early, 2 * WIN), :]

    @pl.when(core != 0)
    def _():
        late_s[pl.ds(0, WIN), :] = own_ref[pl.ds(rows - WIN, WIN), :]
        late_s[pl.ds(WIN, WIN), :] = jnp.where(position == devices - 1, tail_ref[...], halo_ref[pl.ds(0, WIN), :])

    lane = lax.broadcasted_iota(jnp.int32, (1, LANES), 1)
    reach = tiles + 1 + WIN
    begins = []
    for band in range(bands):
        start = starts_ref[band]
        begin = jnp.where(is_col, BEFORE * LANES - (OFF_DEV - 1) - start, start)
        begins.append(begin)
        whole, part = begin // LANES, begin % LANES
        here = pair_s[pl.ds(whole, reach), :]
        below = pair_s[pl.ds(whole + 1, reach), :]
        shifted[band, pl.ds(0, reach), :] = pltpu.roll(jnp.where(lane < part, below, here), LANES - part, 1)
    center, spread = window_moments(shifted[...].reshape(-1, LANES), shift_s)
    center_s[...] = center.reshape(center_s.shape)
    factor_s[...] = lax.rsqrt(spread + M * EPS).reshape(factor_s.shape)
    late_center, late_spread = window_moments(late_s[...], shift_s)
    late_factor = lax.rsqrt(late_spread + M * EPS)

    ahead, near_part = tile_masks()

    for band in range(bands):
        lines = [turned(shifted[band, pl.ds(row, 1), :]) for row in range(WIN + 1)]
        sheets = [sheet(a, b, ahead) for a, b in zip(lines, lines[1:])]
        turned_s[band] = lines[-1]
        sheet_s[band] = sheets[-1]
        pair_z_s[band] = centered(*sheets, center_s[band, pl.ds(0, 1), :], factor_s[band, pl.ds(0, 1), :])

    shift = core * tiles * LANES
    low_edge = BEFORE * LANES - (position - distance) * block - shift
    high_edge = (devices - position - distance) * block - shift
    lo = jnp.where(is_col, low_edge, 0)
    hi = jnp.where(is_col, 1 << 30, high_edge)

    lines = [turned(late_s[pl.ds(row, 1), :]) for row in range(2 * WIN)]
    sheets = [sheet(a, b, ahead) for a, b in zip(lines, lines[1:])]
    for tile in range(WIN):
        late_z_s[tile] = jnp.transpose(centered(sheets[tile], sheets[tile + 1], late_center[tile : tile + 1]))

    def steps(masked, group, _):
        lines = [turned_s[band] for band in range(bands)]
        sheets = [sheet_s[band] for band in range(bands)]
        pairs = [pair_z_s[band] for band in range(bands)]
        for inner in range(unroll):
            tile = group * unroll + inner
            own = z_ref[tile]
            if inner >= unroll - WIN:
                own = jnp.where(group == groups - 1, late_z_s[inner + WIN - unroll], own)
            best = None
            for band in range(bands):
                at = tile + 1
                line = turned(shifted[band, pl.ds(at + WIN, 1), :])
                high = sheet(lines[band], line, ahead)
                following = centered(
                    sheets[band], high, center_s[band, pl.ds(at, 1), :], factor_s[band, pl.ds(at, 1), :]
                )
                lines[band], sheets[band] = line, high
                both = jnp.concatenate([pairs[band], following], axis=1)
                pairs[band] = following
                scores = jnp.dot(own, both, preferred_element_type=jnp.float32)
                if masked:
                    index = begins[band] + tile * LANES + lax.broadcasted_iota(jnp.int32, (1, 2 * LANES), 1)
                    scores = jnp.where((index >= lo) & (index < hi), scores, -1e30)
                mixed = jnp.where(near_part, scores[:, :LANES], scores[:, LANES:])
                best = mixed if best is None else jnp.maximum(best, mixed)
            found = jnp.max(best, axis=1, keepdims=True)
            best_s[...] = jnp.where(lane == tile, found, best_s[...])
        for band in range(bands):
            turned_s[band] = lines[band]
            sheet_s[band] = sheets[band]
            pair_z_s[band] = pairs[band]
        return 0

    size = unroll * LANES
    first_full, last_full = jnp.int32(0), jnp.int32(groups)
    for begin in begins:
        first_full = jnp.maximum(first_full, (lo - begin + size - 1) // size)
        last_full = jnp.minimum(last_full, (hi - begin - LANES) // size)
    first_full = jnp.clip(first_full, 0, groups)
    last_full = jnp.clip(last_full, first_full, groups)
    lax.fori_loop(0, first_full, functools.partial(steps, True), 0)
    lax.fori_loop(first_full, last_full, functools.partial(steps, False), 0)
    lax.fori_loop(last_full, groups, functools.partial(steps, True), 0)
    found = jnp.transpose(best_s[...])[:tiles]
    out_ref[...] = jnp.maximum(found * factor_ref[...], -1.0)
    late = jnp.maximum(found[early:] * late_factor[:WIN], -1.0)
    out_ref[pl.ds(early, WIN), :] = late


def profile(geometry, starts, own, halo, tail, main, side, factor, z):
    devices, distance, rows, tiles, role = geometry
    bands = starts.shape[0]
    vmem = pl.BlockSpec(memory_space=pltpu.VMEM)
    pad = -(-(tiles + 2 + WIN) // 8) * 8
    return pl.pallas_call(
        functools.partial(profile_kernel, geometry + (UNROLL,)),
        out_shape=jax.ShapeDtypeStruct((tiles, LANES), jnp.float32),
        in_specs=[pl.BlockSpec(memory_space=pltpu.SMEM)] + [vmem] * 7,
        out_specs=vmem,
        scratch_shapes=[
            pltpu.VMEM((WIN, LANES, M), jnp.bfloat16),
            pltpu.VMEM((8, LANES), jnp.float32),
            pltpu.VMEM((-(-(tiles + AFTER + 8) // 8) * 8, LANES), jnp.float32),
            pltpu.VMEM((bands, pad, LANES), jnp.float32),
            pltpu.VMEM((bands, pad, LANES), jnp.float32),
            pltpu.VMEM((bands, pad, LANES), jnp.float32),
            pltpu.VMEM((STEPS, bands * pad + 8, LANES), jnp.float32),
            pltpu.VMEM((bands, LANES, LANES), jnp.float32),
            pltpu.VMEM((bands, LANES, LANES), jnp.float32),
            pltpu.VMEM((bands, M, LANES), jnp.bfloat16),
            pltpu.VMEM((LANES, LANES), jnp.float32),
        ],
        compiler_params=pltpu.CompilerParams(vmem_limit_bytes=VMEM_LIMIT),
    )(starts, own, halo, tail, main, side, factor, z)


def body(series, tail, band_starts):
    block_len = series.shape[0]
    rows = block_len // LANES
    devices, cores = lax.axis_size("tm"), lax.axis_size("band")
    distance = BAND_BASE // block_len
    tiles = rows // cores
    position, core = lax.axis_index("tm"), lax.axis_index("band")
    own = series.reshape(rows, LANES)
    tail = tail.reshape(WIN, LANES)

    def move(value, steps):
        route = [
            ((d + s) * cores + c, d * cores + c) for d, c, s in steps if 0 <= d + s < devices
        ]
        return lax.ppermute(value, ("tm", "band"), route)

    row_side = range(devices - distance)
    col_side = range(distance, devices)
    main_row = [(d, c, distance) for d in row_side for c in range(cores)]
    main_col = [(d, c, -distance) for d in col_side for c in range(cores)]
    side_row = [(d, 1, distance + 1) for d in row_side]
    side_col = [(d, 0, -distance - 1) for d in col_side] + [(d, 1, 1 - distance) for d in col_side]
    merged = devices <= 2 * distance
    roles = [(None, main_row + main_col, side_row + side_col)] if merged else [
        (False, main_row, side_row),
        (True, main_col, side_col),
    ]
    mains = [move(own, pairs) for _, pairs, _ in roles]
    edge = lax.dynamic_slice_in_dim(own, jnp.where(core == 0, rows - AFTER, 0), AFTER)
    sides = [move(edge, pairs) for _, _, pairs in roles]
    halo = move(edge, [(d, 1, 1) for d in range(devices)])
    z, factor = own_side(tiles, own)
    found = []
    for (role, _, _), main, side in zip(roles, mains, sides):
        part = profile((devices, distance, rows, tiles, role), band_starts, own, halo, tail, main, side, factor, z)
        other = lax.ppermute(part, "band", [(0, 1), (1, 0)])
        mine = jnp.arange(cores)[:, None, None] == core
        found.append(jnp.where(mine, part[None], other[None]).reshape(-1))
    row_best = jnp.where(position < devices - distance, found[0], -1.0)
    col_best = jnp.where(position >= distance, found[-1], -1.0)
    return row_best, col_best


UNROLL = 8
VMEM_LIMIT = 24 << 20


def solution(mesh):
    placed = (P(("groups", "tm")), P("groups"), P("groups"))
    return jax.shard_map(
        body,
        mesh=mesh,
        in_specs=placed,
        out_specs=(P(("groups", "tm")), P(("groups", "tm"))),
        check_vma=False,
    )
```

```python
import functools

import jax
import jax.numpy as jnp
from jax import lax
from jax.experimental import pallas as pl
from jax.experimental.pallas import tpu as pltpu
from jax.sharding import PartitionSpec as P

M = 256
LANES = 128
OFF_DEV = 128
BAND_SPAN = 4096
BAND_BASE = 65536
EPS = 1e-06

WIN = M // LANES
BEFORE = BAND_SPAN // LANES + 1
AFTER = BEFORE + WIN


def window_moments(samples, scratch):
    count = samples.shape[0]
    lane = lax.broadcasted_iota(jnp.int32, samples.shape, 1)
    slots = iter(range(scratch.shape[0]))

    def ahead(values, distance):
        slot = next(slots)
        scratch[slot, pl.ds(0, count), :] = values
        below = scratch[slot, pl.ds(1, count), :]
        if distance == LANES:
            return below
        joined = jnp.where(lane < distance, below, values)
        return pltpu.roll(joined, LANES - distance, 1)

    total = samples
    spread = None
    size = 1
    while size < M:
        later = ahead(total, size)
        gap = later - total
        step = gap * gap * (0.5 / size)
        spread = step if spread is None else spread + ahead(spread, size) + step
        total = later + total
        size *= 2
    return total * (1.0 / M), spread


STEPS = 15


def tile_masks():
    row_id = lax.broadcasted_iota(jnp.int32, (LANES, LANES), 0)
    col_id = lax.broadcasted_iota(jnp.int32, (LANES, LANES), 1)
    return col_id > row_id, col_id >= row_id


def turned(line):
    return pltpu.roll(jnp.broadcast_to(line, (LANES, LANES)), 1, 1, stride=1, stride_axis=0)


def sheet(before, after, ahead):
    return jnp.where(ahead, after, before)


def centered(low, high, center, factor=None):
    low, high = low - center, high - center
    if factor is not None:
        low, high = low * factor, high * factor
    return jnp.concatenate([low.astype(jnp.bfloat16), high.astype(jnp.bfloat16)], axis=0)


def backwards(rows):
    lane = lax.broadcasted_iota(jnp.int32, rows.shape, 1)
    return jnp.take_along_axis(rows, LANES - 1 - lane, axis=1)


def turned_back(line):
    return pltpu.roll(jnp.broadcast_to(line, (LANES, LANES)), 0, 1, stride=1, stride_axis=0)


def own_tile(low, high, center):
    return jnp.concatenate([(low - center).astype(jnp.bfloat16), (high - center).astype(jnp.bfloat16)], axis=1)


def parts(values):
    first = values.astype(jnp.bfloat16)
    rest = values - first.astype(jnp.float32)
    second = rest.astype(jnp.bfloat16)
    return first, second, (rest - second.astype(jnp.float32)).astype(jnp.bfloat16)


def own_kernel(
    tiles,
    unroll,
    starts_hbm,
    tail_hbm,
    own_hbm,
    z_ref,
    factor_ref,
    own_ref,
    tail_ref,
    starts_ref,
    rows_s,
    back_s,
    center_s,
    shift_s,
    pick_s,
    turned_s,
    sheet_s,
    sem,
):
    copies = [
        pltpu.make_async_copy(own_hbm, own_ref, sem.at[0]),
        pltpu.make_async_copy(tail_hbm, tail_ref, sem.at[1]),
        pltpu.make_async_copy(starts_hbm, starts_ref, sem.at[2]),
    ]
    for copy in copies:
        copy.start()
    first_row = lax.axis_index("band") * tiles
    count = rows_s.shape[0]
    pick_s[...] = jnp.where(lax.broadcasted_iota(jnp.int32, pick_s.shape, 0) == LANES, 1.0, 0.0)
    center_s[...] = jnp.zeros(center_s.shape, jnp.float32)
    rows_s[pl.ds(tiles, count - tiles), :] = jnp.zeros((count - tiles, LANES), jnp.float32)
    for copy in copies:
        copy.wait()
    rows_s[pl.ds(0, tiles), :] = own_ref[pl.ds(first_row, tiles), :]

    @pl.when(first_row == 0)
    def _():
        rows_s[pl.ds(tiles, WIN), :] = own_ref[pl.ds(tiles, WIN), :]

    samples = rows_s[...]
    back_s[...] = backwards(samples)
    center, spread = window_moments(samples, shift_s)
    factor_ref[...] = lax.rsqrt(spread + M * EPS)[:tiles]
    center_s[pl.ds(0, tiles), :] = center[:tiles]
    columns = jnp.concatenate(parts(jnp.transpose(center_s[...])), axis=1)
    _, straight = tile_masks()
    first, second = (turned_back(back_s[pl.ds(row, 1), :]) for row in range(2))
    turned_s[...] = second
    sheet_s[...] = sheet(second, first, straight)

    def group(index, _):
        line, low = turned_s[...], sheet_s[...]
        for pair in range(unroll // 2):
            tile = index * unroll + 2 * pair
            pick = jnp.concatenate(
                [pick_s[pl.ds(LANES - tile - t, LANES), :].astype(jnp.bfloat16) for t in range(2)], axis=1
            )
            spreads = jnp.dot(columns, jnp.concatenate([pick] * 3, axis=0), preferred_element_type=jnp.float32)
            for t in range(2):
                after = turned_back(back_s[pl.ds(tile + t + 2, 1), :])
                high = sheet(after, line, straight)
                z_ref[tile + t] = own_tile(low, high, spreads[:, t * LANES : (t + 1) * LANES])
                line, low = after, high
        turned_s[...] = line
        sheet_s[...] = low
        return 0

    lax.fori_loop(0, tiles // unroll, group, 0)


def own_side(tiles, starts, tail, own):
    vmem = pl.BlockSpec(memory_space=pltpu.VMEM)
    count = -(-(tiles + WIN) // 8) * 8
    return pl.pallas_call(
        functools.partial(own_kernel, tiles, OWN_UNROLL),
        out_shape=(
            jax.ShapeDtypeStruct((tiles, LANES, M), jnp.bfloat16),
            jax.ShapeDtypeStruct((tiles, LANES), jnp.float32),
            jax.ShapeDtypeStruct(own.shape, own.dtype),
            jax.ShapeDtypeStruct(tail.shape, tail.dtype),
            jax.ShapeDtypeStruct(starts.shape, starts.dtype),
        ),
        in_specs=[pl.BlockSpec(memory_space=pltpu.HBM)] * 3,
        out_specs=(vmem, vmem, vmem, vmem, pl.BlockSpec(memory_space=pltpu.SMEM)),
        scratch_shapes=[
            pltpu.VMEM((count, LANES), jnp.float32),
            pltpu.VMEM((count, LANES), jnp.float32),
            pltpu.VMEM((LANES, LANES), jnp.float32),
            pltpu.VMEM((STEPS, count + 8, LANES), jnp.float32),
            pltpu.VMEM((2 * LANES, LANES), jnp.float32),
            pltpu.VMEM((LANES, LANES), jnp.float32),
            pltpu.VMEM((LANES, LANES), jnp.float32),
            pltpu.SemaphoreType.DMA((3,)),
        ],
        compiler_params=pltpu.CompilerParams(vmem_limit_bytes=VMEM_LIMIT),
        cost_estimate=pl.CostEstimate(flops=20 * tiles * LANES * M, transcendentals=0, bytes_accessed=2 * tiles * LANES * M),
    )(starts, tail, own)


def profile_kernel(
    geometry,
    starts_ref,
    own_ref,
    halo_ref,
    tail_ref,
    main_ref,
    side_ref,
    factor_ref,
    z_ref,
    out_ref,
    late_z_s,
    late_s,
    pair_s,
    shifted,
    center_s,
    factor_s,
    shift_s,
    turned_s,
    sheet_s,
    even_z_s,
    odd_z_s,
    before_even_s,
    before_odd_s,
    best_s,
):
    devices, distance, rows, tiles, role, unroll = geometry
    bands = starts_ref.shape[0]
    position = lax.axis_index("tm")
    core = lax.axis_index("band")
    is_col = position >= distance if role is None else jnp.bool_(role)
    block = rows * LANES
    groups = tiles // unroll
    early = tiles - WIN

    pair_s[pl.ds(tiles + AFTER, pair_s.shape[0] - tiles - AFTER), :] = jnp.zeros(
        (pair_s.shape[0] - tiles - AFTER, LANES), jnp.float32
    )

    @pl.when(jnp.logical_not(is_col) & (core == 0))
    def _():
        pair_s[pl.ds(0, tiles + AFTER), :] = main_ref[pl.ds(0, tiles + AFTER), :]

    @pl.when(jnp.logical_not(is_col) & (core != 0))
    def _():
        pair_s[pl.ds(0, tiles), :] = main_ref[pl.ds(rows - tiles, tiles), :]
        pair_s[pl.ds(tiles, AFTER), :] = side_ref[...]

        @pl.when(position == devices - distance - 1)
        def _():
            pair_s[pl.ds(tiles, WIN), :] = tail_ref[...]

    @pl.when(is_col & (core == 0))
    def _():
        pair_s[pl.ds(0, BEFORE), :] = side_ref[pl.ds(WIN, BEFORE), :]
        pair_s[pl.ds(BEFORE, tiles + WIN), :] = main_ref[pl.ds(0, tiles + WIN), :]

    @pl.when(is_col & (core != 0))
    def _():
        pair_s[pl.ds(0, tiles + BEFORE), :] = main_ref[pl.ds(rows - tiles - BEFORE, tiles + BEFORE), :]
        pair_s[pl.ds(tiles + BEFORE, WIN), :] = side_ref[pl.ds(0, WIN), :]

    @pl.when(core == 0)
    def _():
        late_s[pl.ds(0, 2 * WIN), :] = own_ref[pl.ds(early, 2 * WIN), :]

    @pl.when(core != 0)
    def _():
        late_s[pl.ds(0, WIN), :] = own_ref[pl.ds(rows - WIN, WIN), :]
        late_s[pl.ds(WIN, WIN), :] = jnp.where(position == devices - 1, tail_ref[...], halo_ref[pl.ds(0, WIN), :])

    lane = lax.broadcasted_iota(jnp.int32, (1, LANES), 1)
    reach = tiles + 1 + WIN
    begins = []
    for band in range(bands):
        start = starts_ref[band]
        begin = jnp.where(is_col, BEFORE * LANES - (OFF_DEV - 1) - start, start)
        begins.append(begin)
        whole, part = begin // LANES, begin % LANES
        here = pair_s[pl.ds(whole, reach), :]
        below = pair_s[pl.ds(whole + 1, reach), :]
        shifted[band, pl.ds(0, reach), :] = pltpu.roll(jnp.where(lane < part, below, here), LANES - part, 1)
    center, spread = window_moments(shifted[...].reshape(-1, LANES), shift_s)
    center_s[...] = center.reshape(center_s.shape)
    factor_s[...] = lax.rsqrt(spread + M * EPS).reshape(factor_s.shape)
    late_center, late_spread = window_moments(late_s[...], shift_s)
    late_factor = lax.rsqrt(late_spread + M * EPS)

    ahead, near_part = tile_masks()

    half = unroll // PHASES

    def prepare(first, buffer, last_ref):
        for band in range(bands):
            line, low = turned_s[band], sheet_s[band]
            for inner in range(half):
                at = first + 1 + inner
                after = turned(shifted[band, pl.ds(at + WIN, 1), :])
                high = sheet(line, after, ahead)
                z = centered(low, high, center_s[band, pl.ds(at, 1), :], factor_s[band, pl.ds(at, 1), :])
                buffer[band, inner] = z
                line, low = after, high
            last_ref[band] = z
            turned_s[band] = line
            sheet_s[band] = low

    for band in range(bands):
        lines = [turned(shifted[band, pl.ds(row, 1), :]) for row in range(WIN + 1)]
        sheets = [sheet(a, b, ahead) for a, b in zip(lines, lines[1:])]
        turned_s[band] = lines[-1]
        sheet_s[band] = sheets[-1]
        before_even_s[band] = centered(*sheets, center_s[band, pl.ds(0, 1), :], factor_s[band, pl.ds(0, 1), :])
    prepare(0, even_z_s, before_odd_s)

    shift = core * tiles * LANES
    low_edge = BEFORE * LANES - (position - distance) * block - shift
    high_edge = (devices - position - distance) * block - shift
    lo = jnp.where(is_col, low_edge, 0)
    hi = jnp.where(is_col, 1 << 30, high_edge)

    back = backwards(late_s[...])
    lines = [turned_back(back[row : row + 1]) for row in range(2 * WIN)]
    sheets = [sheet(b, a, near_part) for a, b in zip(lines, lines[1:])]
    for tile in range(WIN):
        spread_out = jnp.transpose(jnp.broadcast_to(late_center[tile : tile + 1], (LANES, LANES)))
        late_z_s[tile] = own_tile(sheets[tile], sheets[tile + 1], spread_out)

    def products(masked, group, phase, before, buffer):
        first = group * unroll + phase * half
        for inner in range(half):
            tile = first + inner
            own = z_ref[tile]
            tile_in_group = phase * half + inner
            late = tile_in_group - (unroll - WIN)
            if late >= 0:
                own = jnp.where(group == groups - 1, late_z_s[late], own)
            best = None
            for band in range(bands):
                here = before[band] if inner == 0 else buffer[band, inner - 1]
                both = jnp.concatenate([here, buffer[band, inner]], axis=1)
                scores = jnp.dot(own, both, preferred_element_type=jnp.float32)
                if masked:
                    index = begins[band] + tile * LANES + lax.broadcasted_iota(jnp.int32, (1, 2 * LANES), 1)
                    scores = jnp.where((index >= lo) & (index < hi), scores, -1e30)
                mixed = jnp.where(near_part, scores[:, :LANES], scores[:, LANES:])
                best = mixed if best is None else jnp.maximum(best, mixed)
            best_s[tile] = best

    def steps(masked, group, _):
        first = group * unroll
        for phase in range(PHASES):
            before, buffer, other, other_buffer = (
                (before_even_s, even_z_s, before_odd_s, odd_z_s)
                if phase % 2 == 0
                else (before_odd_s, odd_z_s, before_even_s, even_z_s)
            )
            at = first + phase * half
            products(masked, group, phase, before, buffer)
            prepare(at + half, other_buffer, before)
        return 0

    size = unroll * LANES
    first_full, last_full = jnp.int32(0), jnp.int32(groups)
    for begin in begins:
        first_full = jnp.maximum(first_full, (lo - begin + size - 1) // size)
        last_full = jnp.minimum(last_full, (hi - begin - LANES) // size)
    first_full = jnp.clip(first_full, 0, groups)
    last_full = jnp.clip(last_full, first_full, groups)
    lax.fori_loop(0, first_full, functools.partial(steps, True), 0)
    lax.fori_loop(first_full, last_full, functools.partial(steps, False), 0)
    lax.fori_loop(last_full, groups, functools.partial(steps, True), 0)

    def reduce(group, columns):
        for inner in range(unroll):
            tile = group * unroll + inner
            columns = jnp.where(lane == tile, jnp.max(best_s[tile], axis=1, keepdims=True), columns)
        return columns

    columns = lax.fori_loop(0, groups, reduce, jnp.zeros((LANES, LANES), jnp.float32))
    found = jnp.transpose(columns)[:tiles]
    out_ref[...] = jnp.maximum(found * factor_ref[...], -1.0)
    late = jnp.maximum(found[early:] * late_factor[:WIN], -1.0)
    out_ref[pl.ds(early, WIN), :] = late


def profile(geometry, starts, own, halo, tail, main, side, factor, z):
    devices, distance, rows, tiles, role = geometry
    bands = starts.shape[0]
    vmem = pl.BlockSpec(memory_space=pltpu.VMEM)
    pad = -(-(tiles + UNROLL // PHASES + 1 + WIN) // 8) * 8
    return pl.pallas_call(
        functools.partial(profile_kernel, geometry + (UNROLL,)),
        out_shape=jax.ShapeDtypeStruct((tiles, LANES), jnp.float32),
        in_specs=[pl.BlockSpec(memory_space=pltpu.SMEM)] + [vmem] * 7,
        out_specs=vmem,
        scratch_shapes=[
            pltpu.VMEM((WIN, LANES, M), jnp.bfloat16),
            pltpu.VMEM((8, LANES), jnp.float32),
            pltpu.VMEM((-(-(tiles + AFTER + 8) // 8) * 8, LANES), jnp.float32),
            pltpu.VMEM((bands, pad, LANES), jnp.float32),
            pltpu.VMEM((bands, pad, LANES), jnp.float32),
            pltpu.VMEM((bands, pad, LANES), jnp.float32),
            pltpu.VMEM((STEPS, bands * pad + 8, LANES), jnp.float32),
            pltpu.VMEM((bands, LANES, LANES), jnp.float32),
            pltpu.VMEM((bands, LANES, LANES), jnp.float32),
            pltpu.VMEM((bands, UNROLL // PHASES, M, LANES), jnp.bfloat16),
            pltpu.VMEM((bands, UNROLL // PHASES, M, LANES), jnp.bfloat16),
            pltpu.VMEM((bands, M, LANES), jnp.bfloat16),
            pltpu.VMEM((bands, M, LANES), jnp.bfloat16),
            pltpu.VMEM((tiles, LANES, LANES), jnp.float32),
        ],
        compiler_params=pltpu.CompilerParams(vmem_limit_bytes=VMEM_LIMIT),
    )(starts, own, halo, tail, main, side, factor, z)


def body(series, tail, band_starts):
    block_len = series.shape[0]
    rows = block_len // LANES
    devices, cores = lax.axis_size("tm"), lax.axis_size("band")
    distance = BAND_BASE // block_len
    tiles = rows // cores
    position, core = lax.axis_index("tm"), lax.axis_index("band")
    own = series.reshape(rows, LANES)
    tail = tail.reshape(WIN, LANES)

    def move(value, steps):
        route = [
            ((d + s) * cores + c, d * cores + c) for d, c, s in steps if 0 <= d + s < devices
        ]
        return lax.ppermute(value, ("tm", "band"), route)

    row_side = range(devices - distance)
    col_side = range(distance, devices)
    main_row = [(d, c, distance) for d in row_side for c in range(cores)]
    main_col = [(d, c, -distance) for d in col_side for c in range(cores)]
    side_row = [(d, 1, distance + 1) for d in row_side]
    side_col = [(d, 0, -distance - 1) for d in col_side] + [(d, 1, 1 - distance) for d in col_side]
    merged = devices <= 2 * distance
    roles = [(None, main_row + main_col, side_row + side_col)] if merged else [
        (False, main_row, side_row),
        (True, main_col, side_col),
    ]
    mains = [move(own, pairs) for _, pairs, _ in roles]
    edge = lax.dynamic_slice_in_dim(own, jnp.where(core == 0, rows - AFTER, 0), AFTER)
    sides = [move(edge, pairs) for _, _, pairs in roles]
    halo = move(edge, [(d, 1, 1) for d in range(devices)])
    in_hbm = [pltpu.with_memory_space_constraint(value, pltpu.HBM) for value in (band_starts, tail, own)]
    z, factor, own, tail, starts = own_side(tiles, *in_hbm)
    found = []
    for (role, _, _), main, side in zip(roles, mains, sides):
        part = profile((devices, distance, rows, tiles, role), starts, own, halo, tail, main, side, factor, z)
        other = lax.ppermute(part, "band", [(0, 1), (1, 0)])
        mine = jnp.arange(cores)[:, None, None] == core
        found.append(jnp.where(mine, part[None], other[None]).reshape(-1))
    row_best = jnp.where(position < devices - distance, found[0], -1.0)
    col_best = jnp.where(position >= distance, found[-1], -1.0)
    return row_best, col_best


UNROLL = 16
OWN_UNROLL = 8
PHASES = 8
VMEM_LIMIT = 24 << 20


def solution(mesh):
    placed = (P(("groups", "tm")), P("groups"), P("groups"))
    return jax.shard_map(
        body,
        mesh=mesh,
        in_specs=placed,
        out_specs=(P(("groups", "tm")), P(("groups", "tm"))),
        check_vma=False,
    )
```

```python
import functools

import jax
import jax.numpy as jnp
from jax import lax
from jax.experimental import pallas as pl
from jax.experimental.pallas import tpu as pltpu
from jax.sharding import PartitionSpec as P


M = 256
LANES = 128
OFF_DEV = 128
BAND_SPAN = 4096
BAND_BASE = 65536
EPS = 1e-06

WIN = M // LANES
BEFORE = BAND_SPAN // LANES + 1
AFTER = BEFORE + WIN


def window_moments(samples, scratch):
    count = samples.shape[0]
    lane = lax.broadcasted_iota(jnp.int32, samples.shape, 1)
    slots = iter(range(scratch.shape[0]))

    def ahead(values, distance):
        slot = next(slots)
        scratch[slot, pl.ds(0, count), :] = values
        below = scratch[slot, pl.ds(1, count), :]
        if distance == LANES:
            return below
        joined = jnp.where(lane < distance, below, values)
        return pltpu.roll(joined, LANES - distance, 1)

    total = samples
    spread = None
    size = 1
    while size < M:
        later = ahead(total, size)
        gap = later - total
        step = gap * gap * (0.5 / size)
        spread = step if spread is None else spread + ahead(spread, size) + step
        total = later + total
        size *= 2
    return total * (1.0 / M), spread


STEPS = 15


def tile_masks():
    row_id = lax.broadcasted_iota(jnp.int32, (LANES, LANES), 0)
    col_id = lax.broadcasted_iota(jnp.int32, (LANES, LANES), 1)
    return col_id > row_id, col_id >= row_id


def turned(line):
    return pltpu.roll(jnp.broadcast_to(line, (LANES, LANES)), 1, 1, stride=1, stride_axis=0)


def sheet(before, after, ahead):
    return jnp.where(ahead, after, before)


def centered(low, high, center, factor=None):
    low, high = low - center, high - center
    if factor is not None:
        low, high = low * factor, high * factor
    return jnp.concatenate([low.astype(jnp.bfloat16), high.astype(jnp.bfloat16)], axis=0)


def backwards(rows):
    lane = lax.broadcasted_iota(jnp.int32, rows.shape, 1)
    return jnp.take_along_axis(rows, LANES - 1 - lane, axis=1)


def turned_back(line):
    return pltpu.roll(jnp.broadcast_to(line, (LANES, LANES)), 0, 1, stride=1, stride_axis=0)


def own_tile(low, high, center):
    return jnp.concatenate([(low - center).astype(jnp.bfloat16), (high - center).astype(jnp.bfloat16)], axis=1)


def parts(values):
    first = values.astype(jnp.bfloat16)
    rest = values - first.astype(jnp.float32)
    second = rest.astype(jnp.bfloat16)
    return first, second, (rest - second.astype(jnp.float32)).astype(jnp.bfloat16)


def own_kernel(
    tiles,
    unroll,
    starts_hbm,
    tail_hbm,
    own_hbm,
    z_ref,
    factor_ref,
    own_ref,
    tail_ref,
    starts_ref,
    rows_s,
    back_s,
    center_s,
    shift_s,
    pick_s,
    turned_s,
    sheet_s,
    sem,
):
    copies = [
        pltpu.make_async_copy(own_hbm, own_ref, sem.at[0]),
        pltpu.make_async_copy(tail_hbm, tail_ref, sem.at[1]),
        pltpu.make_async_copy(starts_hbm, starts_ref, sem.at[2]),
    ]
    for copy in copies:
        copy.start()
    first_row = lax.axis_index("band") * tiles
    count = rows_s.shape[0]
    pick_s[...] = jnp.where(lax.broadcasted_iota(jnp.int32, pick_s.shape, 0) == LANES, 1.0, 0.0)
    center_s[...] = jnp.zeros(center_s.shape, jnp.float32)
    rows_s[pl.ds(tiles, count - tiles), :] = jnp.zeros((count - tiles, LANES), jnp.float32)
    for copy in copies:
        copy.wait()
    rows_s[pl.ds(0, tiles), :] = own_ref[pl.ds(first_row, tiles), :]

    @pl.when(first_row == 0)
    def _():
        rows_s[pl.ds(tiles, WIN), :] = own_ref[pl.ds(tiles, WIN), :]

    samples = rows_s[...]
    back_s[...] = backwards(samples)
    center, spread = window_moments(samples, shift_s)
    factor_ref[...] = lax.rsqrt(spread + M * EPS)[:tiles]
    center_s[pl.ds(0, tiles), :] = center[:tiles]
    columns = jnp.concatenate(parts(jnp.transpose(center_s[...])), axis=1)
    _, straight = tile_masks()
    first, second = (turned_back(back_s[pl.ds(row, 1), :]) for row in range(2))
    turned_s[...] = second
    sheet_s[...] = sheet(second, first, straight)

    def group(index, _):
        line, low = turned_s[...], sheet_s[...]
        for pair in range(unroll // 2):
            tile = index * unroll + 2 * pair
            pick = jnp.concatenate(
                [pick_s[pl.ds(LANES - tile - t, LANES), :].astype(jnp.bfloat16) for t in range(2)], axis=1
            )
            spreads = jnp.dot(columns, jnp.concatenate([pick] * 3, axis=0), preferred_element_type=jnp.float32)
            for t in range(2):
                after = turned_back(back_s[pl.ds(tile + t + 2, 1), :])
                high = sheet(after, line, straight)
                z_ref[tile + t] = own_tile(low, high, spreads[:, t * LANES : (t + 1) * LANES])
                line, low = after, high
        turned_s[...] = line
        sheet_s[...] = low
        return 0

    lax.fori_loop(0, tiles // unroll, group, 0)


def own_side(tiles, starts, tail, own):
    vmem = pl.BlockSpec(memory_space=pltpu.VMEM)
    count = -(-(tiles + WIN) // 8) * 8
    return pl.pallas_call(
        functools.partial(own_kernel, tiles, min(tiles, OWN_UNROLL)),
        out_shape=(
            jax.ShapeDtypeStruct((tiles, LANES, M), jnp.bfloat16),
            jax.ShapeDtypeStruct((tiles, LANES), jnp.float32),
            jax.ShapeDtypeStruct(own.shape, own.dtype),
            jax.ShapeDtypeStruct(tail.shape, tail.dtype),
            jax.ShapeDtypeStruct(starts.shape, starts.dtype),
        ),
        in_specs=[pl.BlockSpec(memory_space=pltpu.HBM)] * 3,
        out_specs=(vmem, vmem, vmem, vmem, pl.BlockSpec(memory_space=pltpu.SMEM)),
        scratch_shapes=[
            pltpu.VMEM((count, LANES), jnp.float32),
            pltpu.VMEM((count, LANES), jnp.float32),
            pltpu.VMEM((LANES, LANES), jnp.float32),
            pltpu.VMEM((STEPS, count + 8, LANES), jnp.float32),
            pltpu.VMEM((2 * LANES, LANES), jnp.float32),
            pltpu.VMEM((LANES, LANES), jnp.float32),
            pltpu.VMEM((LANES, LANES), jnp.float32),
            pltpu.SemaphoreType.DMA((3,)),
        ],
        compiler_params=pltpu.CompilerParams(vmem_limit_bytes=VMEM_LIMIT),
        cost_estimate=pl.CostEstimate(flops=20 * tiles * LANES * M, transcendentals=0, bytes_accessed=2 * tiles * LANES * M),
    )(starts, tail, own)


def profile_kernel(
    geometry,
    starts_ref,
    own_ref,
    halo_ref,
    tail_ref,
    main_ref,
    side_ref,
    factor_ref,
    z_ref,
    out_ref,
    late_z_s,
    late_s,
    pair_s,
    shifted,
    center_s,
    factor_s,
    shift_s,
    turned_s,
    sheet_s,
    even_z_s,
    odd_z_s,
    before_even_s,
    before_odd_s,
    best_s,
):
    devices, distance, rows, tiles, role, unroll = geometry
    bands = starts_ref.shape[0]
    position = lax.axis_index("tm")
    core = lax.axis_index("band")
    is_col = position >= distance if role is None else jnp.bool_(role)
    block = rows * LANES
    groups = tiles // unroll
    early = tiles - WIN

    pair_s[pl.ds(tiles + AFTER, pair_s.shape[0] - tiles - AFTER), :] = jnp.zeros(
        (pair_s.shape[0] - tiles - AFTER, LANES), jnp.float32
    )

    @pl.when(jnp.logical_not(is_col) & (core == 0))
    def _():
        pair_s[pl.ds(0, tiles + AFTER), :] = main_ref[pl.ds(0, tiles + AFTER), :]

    @pl.when(jnp.logical_not(is_col) & (core != 0))
    def _():
        pair_s[pl.ds(0, tiles), :] = main_ref[pl.ds(rows - tiles, tiles), :]
        pair_s[pl.ds(tiles, AFTER), :] = side_ref[pl.ds(0, AFTER), :]

        @pl.when(position == devices - distance - 1)
        def _():
            pair_s[pl.ds(tiles, WIN), :] = tail_ref[...]

    @pl.when(is_col & (core == 0))
    def _():
        pair_s[pl.ds(0, BEFORE), :] = side_ref[pl.ds(rows - BEFORE, BEFORE), :]
        pair_s[pl.ds(BEFORE, tiles + WIN), :] = main_ref[pl.ds(0, tiles + WIN), :]

    @pl.when(is_col & (core != 0))
    def _():
        pair_s[pl.ds(0, tiles + BEFORE), :] = main_ref[pl.ds(rows - tiles - BEFORE, tiles + BEFORE), :]
        pair_s[pl.ds(tiles + BEFORE, WIN), :] = side_ref[pl.ds(0, WIN), :]

    @pl.when(core == 0)
    def _():
        late_s[pl.ds(0, 2 * WIN), :] = own_ref[pl.ds(early, 2 * WIN), :]

    @pl.when(core != 0)
    def _():
        late_s[pl.ds(0, WIN), :] = own_ref[pl.ds(rows - WIN, WIN), :]
        late_s[pl.ds(WIN, WIN), :] = jnp.where(position == devices - 1, tail_ref[...], halo_ref[pl.ds(0, WIN), :])

    lane = lax.broadcasted_iota(jnp.int32, (1, LANES), 1)
    reach = tiles + 1 + WIN
    begins = []
    for band in range(bands):
        start = starts_ref[band]
        begin = jnp.where(is_col, BEFORE * LANES - (OFF_DEV - 1) - start, start)
        begins.append(begin)
        whole, part = begin // LANES, begin % LANES
        here = pair_s[pl.ds(whole, reach), :]
        below = pair_s[pl.ds(whole + 1, reach), :]
        shifted[band, pl.ds(0, reach), :] = pltpu.roll(jnp.where(lane < part, below, here), LANES - part, 1)
    center, spread = window_moments(shifted[...].reshape(-1, LANES), shift_s)
    center_s[...] = center.reshape(center_s.shape)
    factor_s[...] = lax.rsqrt(spread + M * EPS).reshape(factor_s.shape)
    late_center, late_spread = window_moments(late_s[...], shift_s)
    late_factor = lax.rsqrt(late_spread + M * EPS)

    ahead, near_part = tile_masks()

    half = unroll // PHASES

    def prepare(first, buffer, last_ref):
        for band in range(bands):
            line, low = turned_s[band], sheet_s[band]
            for inner in range(half):
                at = first + 1 + inner
                after = turned(shifted[band, pl.ds(at + WIN, 1), :])
                high = sheet(line, after, ahead)
                z = centered(low, high, center_s[band, pl.ds(at, 1), :], factor_s[band, pl.ds(at, 1), :])
                buffer[band, inner] = z
                line, low = after, high
            last_ref[band] = z
            turned_s[band] = line
            sheet_s[band] = low

    for band in range(bands):
        lines = [turned(shifted[band, pl.ds(row, 1), :]) for row in range(WIN + 1)]
        sheets = [sheet(a, b, ahead) for a, b in zip(lines, lines[1:])]
        turned_s[band] = lines[-1]
        sheet_s[band] = sheets[-1]
        before_even_s[band] = centered(*sheets, center_s[band, pl.ds(0, 1), :], factor_s[band, pl.ds(0, 1), :])
    prepare(0, even_z_s, before_odd_s)

    shift = core * tiles * LANES
    low_edge = BEFORE * LANES - (position - distance) * block - shift
    high_edge = (devices - position - distance) * block - shift
    lo = jnp.where(is_col, low_edge, 0)
    hi = jnp.where(is_col, 1 << 30, high_edge)

    back = backwards(late_s[...])
    lines = [turned_back(back[row : row + 1]) for row in range(2 * WIN)]
    sheets = [sheet(b, a, near_part) for a, b in zip(lines, lines[1:])]
    for tile in range(WIN):
        spread_out = jnp.transpose(jnp.broadcast_to(late_center[tile : tile + 1], (LANES, LANES)))
        late_z_s[tile] = own_tile(sheets[tile], sheets[tile + 1], spread_out)

    def products(masked, group, phase, before, buffer):
        first = group * unroll + phase * half
        for inner in range(half):
            tile = first + inner
            own = z_ref[tile]
            tile_in_group = phase * half + inner
            late = tile_in_group - (unroll - WIN)
            if late >= 0:
                own = jnp.where(group == groups - 1, late_z_s[late], own)
            best = None
            for band in range(bands):
                here = before[band] if inner == 0 else buffer[band, inner - 1]
                both = jnp.concatenate([here, buffer[band, inner]], axis=1)
                scores = jnp.dot(own, both, preferred_element_type=jnp.float32)
                if masked:
                    index = begins[band] + tile * LANES + lax.broadcasted_iota(jnp.int32, (1, 2 * LANES), 1)
                    scores = jnp.where((index >= lo) & (index < hi), scores, -1e30)
                mixed = jnp.where(near_part, scores[:, :LANES], scores[:, LANES:])
                best = mixed if best is None else jnp.maximum(best, mixed)
            best_s[tile] = best

    def steps(masked, group, _):
        first = group * unroll
        for phase in range(PHASES):
            before, buffer, _, other_buffer = (
                (before_even_s, even_z_s, before_odd_s, odd_z_s)
                if phase % 2 == 0
                else (before_odd_s, odd_z_s, before_even_s, even_z_s)
            )
            at = first + phase * half
            products(masked, group, phase, before, buffer)
            prepare(at + half, other_buffer, before)
        return 0

    size = unroll * LANES
    first_full, last_full = jnp.int32(0), jnp.int32(groups)
    for begin in begins:
        first_full = jnp.maximum(first_full, (lo - begin + size - 1) // size)
        last_full = jnp.minimum(last_full, (hi - begin - LANES) // size)
    first_full = jnp.clip(first_full, 0, groups)
    last_full = jnp.clip(last_full, first_full, groups)
    lax.fori_loop(0, first_full, functools.partial(steps, True), 0)
    lax.fori_loop(first_full, last_full, functools.partial(steps, False), 0)
    lax.fori_loop(last_full, groups, functools.partial(steps, True), 0)

    def reduce(group, columns):
        for inner in range(unroll):
            tile = group * unroll + inner
            columns = jnp.where(lane == tile, jnp.max(best_s[tile], axis=1, keepdims=True), columns)
        return columns

    columns = lax.fori_loop(0, groups, reduce, jnp.zeros((LANES, LANES), jnp.float32))
    found = jnp.transpose(columns)[:tiles]
    out_ref[...] = jnp.maximum(found * factor_ref[...], -1.0)
    late = jnp.maximum(found[early:] * late_factor[:WIN], -1.0)
    out_ref[pl.ds(early, WIN), :] = late


def profile(geometry, starts, own, halo, tail, main, side, factor, z):
    _, _, _, tiles, _ = geometry
    bands = starts.shape[0]
    vmem = pl.BlockSpec(memory_space=pltpu.VMEM)
    pad = -(-(tiles + UNROLL // PHASES + 1 + WIN) // 8) * 8
    return pl.pallas_call(
        functools.partial(profile_kernel, geometry + (UNROLL,)),
        out_shape=jax.ShapeDtypeStruct((tiles, LANES), jnp.float32),
        in_specs=[pl.BlockSpec(memory_space=pltpu.SMEM)] + [vmem] * 7,
        out_specs=vmem,
        scratch_shapes=[
            pltpu.VMEM((WIN, LANES, M), jnp.bfloat16),
            pltpu.VMEM((8, LANES), jnp.float32),
            pltpu.VMEM((-(-(tiles + AFTER + 8) // 8) * 8, LANES), jnp.float32),
            pltpu.VMEM((bands, pad, LANES), jnp.float32),
            pltpu.VMEM((bands, pad, LANES), jnp.float32),
            pltpu.VMEM((bands, pad, LANES), jnp.float32),
            pltpu.VMEM((STEPS, bands * pad + 8, LANES), jnp.float32),
            pltpu.VMEM((bands, LANES, LANES), jnp.float32),
            pltpu.VMEM((bands, LANES, LANES), jnp.float32),
            pltpu.VMEM((bands, UNROLL // PHASES, M, LANES), jnp.bfloat16),
            pltpu.VMEM((bands, UNROLL // PHASES, M, LANES), jnp.bfloat16),
            pltpu.VMEM((bands, M, LANES), jnp.bfloat16),
            pltpu.VMEM((bands, M, LANES), jnp.bfloat16),
            pltpu.VMEM((tiles, LANES, LANES), jnp.float32),
        ],
        compiler_params=pltpu.CompilerParams(vmem_limit_bytes=VMEM_LIMIT),
    )(starts, own, halo, tail, main, side, factor, z)


def body(series, tail, band_starts):
    block_len = series.shape[0]
    rows = block_len // LANES
    devices, cores = lax.axis_size("tm"), lax.axis_size("band")
    distance = BAND_BASE // block_len
    tiles = rows // cores
    position, core = lax.axis_index("tm"), lax.axis_index("band")
    own = series.reshape(rows, LANES)
    tail = tail.reshape(WIN, LANES)

    def move(value, steps):
        route = [
            ((d + s) * cores + c, d * cores + c) for d, c, s in steps if 0 <= d + s < devices
        ]
        return lax.ppermute(value, ("tm", "band"), route)

    row_side = range(devices - distance)
    col_side = range(distance, devices)
    main_row = [(d, c, distance) for d in row_side for c in range(cores)]
    main_col = [(d, c, -distance) for d in col_side for c in range(cores)]
    side_row = [(d, 1, distance + 1) for d in row_side]
    side_col = [(d, 0, -distance - 1) for d in col_side] + [(d, 1, 1 - distance) for d in col_side]
    merged = devices <= 2 * distance
    roles = [(None, main_row + main_col, side_row + side_col)] if merged else [
        (False, main_row, side_row),
        (True, main_col, side_col),
    ]
    halo = move(own, [(d, 1, 1) for d in range(devices)])
    sides = [move(own, pairs) for _, _, pairs in roles]
    mains = [move(own, pairs) for _, pairs, _ in roles]
    in_hbm = [pltpu.with_memory_space_constraint(value, pltpu.HBM) for value in (band_starts, tail, own)]
    z, factor, own, tail, starts = own_side(tiles, *in_hbm)
    found = []
    for (role, _, _), main, side in zip(roles, mains, sides):
        part = profile((devices, distance, rows, tiles, role), starts, own, halo, tail, main, side, factor, z)
        other = lax.ppermute(part, "band", [(0, 1), (1, 0)])
        mine = jnp.arange(cores)[:, None, None] == core
        found.append(jnp.where(mine, part[None], other[None]).reshape(-1))
    row_best = jnp.where(position < devices - distance, found[0], -1.0)
    col_best = jnp.where(position >= distance, found[-1], -1.0)
    return row_best, col_best


UNROLL = 16
OWN_UNROLL = 64
PHASES = 8
VMEM_LIMIT = 24 << 20


def solution(mesh):
    placed = (P(("groups", "tm")), P("groups"), P("groups"))
    return jax.shard_map(
        body,
        mesh=mesh,
        in_specs=placed,
        out_specs=(P(("groups", "tm")), P(("groups", "tm"))),
        check_vma=False,
    )
```

```python
import functools

import jax
import jax.numpy as jnp
from jax import lax
from jax.experimental import pallas as pl
from jax.experimental.pallas import tpu as pltpu
from jax.sharding import PartitionSpec as P


M = 256
LANES = 128
OFF_DEV = 128
BAND_SPAN = 4096
BAND_BASE = 65536
EPS = 1e-06

WIN = M // LANES
BEFORE = BAND_SPAN // LANES + 1
AFTER = BEFORE + WIN


def window_moments(samples, scratch):
    count = samples.shape[0]
    lane = lax.broadcasted_iota(jnp.int32, samples.shape, 1)
    slots = iter(range(scratch.shape[0]))

    def ahead(values, distance):
        slot = next(slots)
        scratch[slot, pl.ds(0, count), :] = values
        below = scratch[slot, pl.ds(1, count), :]
        if distance == LANES:
            return below
        joined = jnp.where(lane < distance, below, values)
        return pltpu.roll(joined, LANES - distance, 1)

    total = samples
    spread = None
    size = 1
    while size < M:
        later = ahead(total, size)
        gap = later - total
        step = gap * gap * (0.5 / size)
        spread = step if spread is None else spread + ahead(spread, size) + step
        total = later + total
        size *= 2
    return total * (1.0 / M), spread


STEPS = 15


def tile_masks():
    row_id = lax.broadcasted_iota(jnp.int32, (LANES, LANES), 0)
    col_id = lax.broadcasted_iota(jnp.int32, (LANES, LANES), 1)
    return col_id > row_id, col_id >= row_id


def turned(line):
    return pltpu.roll(jnp.broadcast_to(line, (LANES, LANES)), 1, 1, stride=1, stride_axis=0)


def sheet(before, after, ahead):
    return jnp.where(ahead, after, before)


def centered(low, high, center, factor=None):
    low, high = low - center, high - center
    if factor is not None:
        low, high = low * factor, high * factor
    return jnp.concatenate([low.astype(jnp.bfloat16), high.astype(jnp.bfloat16)], axis=0)


def backwards(rows):
    lane = lax.broadcasted_iota(jnp.int32, rows.shape, 1)
    return jnp.take_along_axis(rows, LANES - 1 - lane, axis=1)


def turned_back(line):
    return pltpu.roll(jnp.broadcast_to(line, (LANES, LANES)), 0, 1, stride=1, stride_axis=0)


def own_tile(low, high, center):
    return jnp.concatenate([(low - center).astype(jnp.bfloat16), (high - center).astype(jnp.bfloat16)], axis=1)


def parts(values):
    first = values.astype(jnp.bfloat16)
    rest = values - first.astype(jnp.float32)
    second = rest.astype(jnp.bfloat16)
    return first, second, (rest - second.astype(jnp.float32)).astype(jnp.bfloat16)


def own_kernel(
    tiles,
    unroll,
    starts_hbm,
    tail_hbm,
    own_hbm,
    z_ref,
    factor_ref,
    own_ref,
    tail_ref,
    starts_ref,
    rows_s,
    back_s,
    center_s,
    shift_s,
    pick_s,
    turned_s,
    sheet_s,
    sem,
):
    copies = [
        pltpu.make_async_copy(own_hbm, own_ref, sem.at[0]),
        pltpu.make_async_copy(tail_hbm, tail_ref, sem.at[1]),
        pltpu.make_async_copy(starts_hbm, starts_ref, sem.at[2]),
    ]
    for copy in copies:
        copy.start()
    first_row = lax.axis_index("band") * tiles
    count = rows_s.shape[0]
    pick_s[...] = jnp.where(lax.broadcasted_iota(jnp.int32, pick_s.shape, 0) == LANES, 1.0, 0.0)
    center_s[...] = jnp.zeros(center_s.shape, jnp.float32)
    rows_s[pl.ds(tiles, count - tiles), :] = jnp.zeros((count - tiles, LANES), jnp.float32)
    for copy in copies:
        copy.wait()
    rows_s[pl.ds(0, tiles), :] = own_ref[pl.ds(first_row, tiles), :]

    @pl.when(first_row == 0)
    def _():
        rows_s[pl.ds(tiles, WIN), :] = own_ref[pl.ds(tiles, WIN), :]

    samples = rows_s[...]
    back_s[...] = backwards(samples)
    center, spread = window_moments(samples, shift_s)
    factor_ref[...] = lax.rsqrt(spread + M * EPS)[:tiles]
    center_s[pl.ds(0, tiles), :] = center[:tiles]
    columns = jnp.concatenate(parts(jnp.transpose(center_s[...])), axis=1)
    _, straight = tile_masks()
    first, second = (turned_back(back_s[pl.ds(row, 1), :]) for row in range(2))
    turned_s[...] = second
    sheet_s[...] = sheet(second, first, straight)

    def group(index, _):
        line, low = turned_s[...], sheet_s[...]
        for pair in range(unroll // 2):
            tile = index * unroll + 2 * pair
            pick = jnp.concatenate(
                [pick_s[pl.ds(LANES - tile - t, LANES), :].astype(jnp.bfloat16) for t in range(2)], axis=1
            )
            spreads = jnp.dot(columns, jnp.concatenate([pick] * 3, axis=0), preferred_element_type=jnp.float32)
            for t in range(2):
                after = turned_back(back_s[pl.ds(tile + t + 2, 1), :])
                high = sheet(after, line, straight)
                z_ref[tile + t] = own_tile(low, high, spreads[:, t * LANES : (t + 1) * LANES])
                line, low = after, high
        turned_s[...] = line
        sheet_s[...] = low
        return 0

    lax.fori_loop(0, tiles // unroll, group, 0)


def own_side(tiles, starts, tail, own):
    vmem = pl.BlockSpec(memory_space=pltpu.VMEM)
    count = -(-(tiles + WIN) // 8) * 8
    return pl.pallas_call(
        functools.partial(own_kernel, tiles, min(tiles, OWN_UNROLL)),
        out_shape=(
            jax.ShapeDtypeStruct((tiles, LANES, M), jnp.bfloat16),
            jax.ShapeDtypeStruct((tiles, LANES), jnp.float32),
            jax.ShapeDtypeStruct(own.shape, own.dtype),
            jax.ShapeDtypeStruct(tail.shape, tail.dtype),
            jax.ShapeDtypeStruct(starts.shape, starts.dtype),
        ),
        in_specs=[pl.BlockSpec(memory_space=pltpu.HBM)] * 3,
        out_specs=(vmem, vmem, vmem, vmem, pl.BlockSpec(memory_space=pltpu.SMEM)),
        scratch_shapes=[
            pltpu.VMEM((count, LANES), jnp.float32),
            pltpu.VMEM((count, LANES), jnp.float32),
            pltpu.VMEM((LANES, LANES), jnp.float32),
            pltpu.VMEM((STEPS, count + 8, LANES), jnp.float32),
            pltpu.VMEM((2 * LANES, LANES), jnp.float32),
            pltpu.VMEM((LANES, LANES), jnp.float32),
            pltpu.VMEM((LANES, LANES), jnp.float32),
            pltpu.SemaphoreType.DMA((3,)),
        ],
        compiler_params=pltpu.CompilerParams(vmem_limit_bytes=VMEM_LIMIT),
        cost_estimate=pl.CostEstimate(flops=20 * tiles * LANES * M, transcendentals=0, bytes_accessed=2 * tiles * LANES * M),
    )(starts, tail, own)


def profile_kernel(
    geometry,
    starts_ref,
    own_ref,
    halo_ref,
    tail_ref,
    main_ref,
    side_ref,
    factor_ref,
    z_ref,
    out_ref,
    late_z_s,
    late_s,
    pair_s,
    shifted,
    center_s,
    factor_s,
    shift_s,
    turned_s,
    sheet_s,
    even_z_s,
    odd_z_s,
    before_even_s,
    before_odd_s,
    best_s,
):
    devices, distance, rows, tiles, role, unroll = geometry
    bands = starts_ref.shape[0]
    position = lax.axis_index("tm")
    core = lax.axis_index("band")
    is_col = position >= distance if role is None else jnp.bool_(role)
    block = rows * LANES
    groups = tiles // unroll
    early = tiles - WIN

    pair_s[pl.ds(tiles + AFTER, pair_s.shape[0] - tiles - AFTER), :] = jnp.zeros(
        (pair_s.shape[0] - tiles - AFTER, LANES), jnp.float32
    )

    @pl.when(jnp.logical_not(is_col) & (core == 0))
    def _():
        pair_s[pl.ds(0, tiles + AFTER), :] = main_ref[pl.ds(0, tiles + AFTER), :]

    @pl.when(jnp.logical_not(is_col) & (core != 0))
    def _():
        pair_s[pl.ds(0, tiles), :] = main_ref[pl.ds(rows - tiles, tiles), :]
        pair_s[pl.ds(tiles, AFTER), :] = side_ref[pl.ds(0, AFTER), :]

        @pl.when(position == devices - distance - 1)
        def _():
            pair_s[pl.ds(tiles, WIN), :] = tail_ref[...]

    @pl.when(is_col & (core == 0))
    def _():
        pair_s[pl.ds(0, BEFORE), :] = side_ref[pl.ds(rows - BEFORE, BEFORE), :]
        pair_s[pl.ds(BEFORE, tiles + WIN), :] = main_ref[pl.ds(0, tiles + WIN), :]

    @pl.when(is_col & (core != 0))
    def _():
        pair_s[pl.ds(0, tiles + BEFORE), :] = main_ref[pl.ds(rows - tiles - BEFORE, tiles + BEFORE), :]
        pair_s[pl.ds(tiles + BEFORE, WIN), :] = side_ref[pl.ds(0, WIN), :]

    @pl.when(core == 0)
    def _():
        late_s[pl.ds(0, 2 * WIN), :] = own_ref[pl.ds(early, 2 * WIN), :]

    @pl.when(core != 0)
    def _():
        late_s[pl.ds(0, WIN), :] = own_ref[pl.ds(rows - WIN, WIN), :]
        late_s[pl.ds(WIN, WIN), :] = jnp.where(position == devices - 1, tail_ref[...], halo_ref[pl.ds(0, WIN), :])

    lane = lax.broadcasted_iota(jnp.int32, (1, LANES), 1)
    reach = tiles + 1 + WIN
    begins = []
    for band in range(bands):
        start = starts_ref[band]
        begin = jnp.where(is_col, BEFORE * LANES - (OFF_DEV - 1) - start, start)
        begins.append(begin)
        whole, part = begin // LANES, begin % LANES
        here = pair_s[pl.ds(whole, reach), :]
        below = pair_s[pl.ds(whole + 1, reach), :]
        shifted[band, pl.ds(0, reach), :] = pltpu.roll(jnp.where(lane < part, below, here), LANES - part, 1)
    center, spread = window_moments(shifted[...].reshape(-1, LANES), shift_s)
    center_s[...] = center.reshape(center_s.shape)
    factor_s[...] = lax.rsqrt(spread + M * EPS).reshape(factor_s.shape)
    late_center, late_spread = window_moments(late_s[...], shift_s)
    late_factor = lax.rsqrt(late_spread + M * EPS)

    ahead, near_part = tile_masks()

    half = unroll // PHASES

    def prepare(first, buffer, last_ref):
        for band in range(bands):
            line, low = turned_s[band], sheet_s[band]
            for inner in range(half):
                at = first + 1 + inner
                after = turned(shifted[band, pl.ds(at + WIN, 1), :])
                high = sheet(line, after, ahead)
                z = centered(low, high, center_s[band, pl.ds(at, 1), :], factor_s[band, pl.ds(at, 1), :])
                buffer[band, inner] = z
                line, low = after, high
            last_ref[band] = z
            turned_s[band] = line
            sheet_s[band] = low

    for band in range(bands):
        lines = [turned(shifted[band, pl.ds(row, 1), :]) for row in range(WIN + 1)]
        sheets = [sheet(a, b, ahead) for a, b in zip(lines, lines[1:])]
        turned_s[band] = lines[-1]
        sheet_s[band] = sheets[-1]
        before_even_s[band] = centered(*sheets, center_s[band, pl.ds(0, 1), :], factor_s[band, pl.ds(0, 1), :])
    prepare(0, even_z_s, before_odd_s)

    shift = core * tiles * LANES
    low_edge = BEFORE * LANES - (position - distance) * block - shift
    high_edge = (devices - position - distance) * block - shift
    lo = jnp.where(is_col, low_edge, 0)
    hi = jnp.where(is_col, 1 << 30, high_edge)

    back = backwards(late_s[...])
    lines = [turned_back(back[row : row + 1]) for row in range(2 * WIN)]
    sheets = [sheet(b, a, near_part) for a, b in zip(lines, lines[1:])]
    for tile in range(WIN):
        spread_out = jnp.transpose(jnp.broadcast_to(late_center[tile : tile + 1], (LANES, LANES)))
        late_z_s[tile] = own_tile(sheets[tile], sheets[tile + 1], spread_out)

    def products(masked, group, phase, before, buffer):
        first = group * unroll + phase * half
        for inner in range(half):
            tile = first + inner
            own = z_ref[tile]
            tile_in_group = phase * half + inner
            late = tile_in_group - (unroll - WIN)
            if late >= 0:
                own = jnp.where(group == groups - 1, late_z_s[late], own)
            best = None
            for band in range(bands):
                here = before[band] if inner == 0 else buffer[band, inner - 1]
                both = jnp.concatenate([here, buffer[band, inner]], axis=1)
                scores = jnp.dot(own, both, preferred_element_type=jnp.float32)
                if masked:
                    index = begins[band] + tile * LANES + lax.broadcasted_iota(jnp.int32, (1, 2 * LANES), 1)
                    scores = jnp.where((index >= lo) & (index < hi), scores, -1e30)
                mixed = jnp.where(near_part, scores[:, :LANES], scores[:, LANES:])
                best = mixed if best is None else jnp.maximum(best, mixed)
            best_s[tile] = best

    def steps(masked, group):
        first = group * unroll
        for phase in range(PHASES):
            before, buffer, _, other_buffer = (
                (before_even_s, even_z_s, before_odd_s, odd_z_s)
                if phase % 2 == 0
                else (before_odd_s, odd_z_s, before_even_s, even_z_s)
            )
            at = first + phase * half
            products(masked, group, phase, before, buffer)
            prepare(at + half, other_buffer, before)
        return 0

    size = unroll * LANES
    first_full, last_full = jnp.int32(0), jnp.int32(groups)
    for begin in begins:
        first_full = jnp.maximum(first_full, (lo - begin + size - 1) // size)
        last_full = jnp.minimum(last_full, (hi - begin - LANES) // size)
    first_full = jnp.clip(first_full, 0, groups)
    last_full = jnp.clip(last_full, first_full, groups)

    def either(group, _):
        full = (group >= first_full) & (group < last_full)

        @pl.when(full)
        def _():
            steps(False, group)

        @pl.when(jnp.logical_not(full))
        def _():
            steps(True, group)

        return 0

    lax.fori_loop(0, groups, either, 0)

    together = min(tiles, REDUCE)

    def reduce(group, columns):
        for inner in range(together):
            tile = group * together + inner
            columns = jnp.where(lane == tile, jnp.max(best_s[tile], axis=1, keepdims=True), columns)
        return columns

    columns = lax.fori_loop(0, tiles // together, reduce, jnp.zeros((LANES, LANES), jnp.float32))
    found = jnp.transpose(columns)[:tiles]
    out_ref[...] = jnp.maximum(found * factor_ref[...], -1.0)
    late = jnp.maximum(found[early:] * late_factor[:WIN], -1.0)
    out_ref[pl.ds(early, WIN), :] = late


def profile(geometry, starts, own, halo, tail, main, side, factor, z):
    _, _, _, tiles, _ = geometry
    bands = starts.shape[0]
    vmem = pl.BlockSpec(memory_space=pltpu.VMEM)
    pad = -(-(tiles + UNROLL // PHASES + 1 + WIN) // 8) * 8
    return pl.pallas_call(
        functools.partial(profile_kernel, geometry + (UNROLL,)),
        out_shape=jax.ShapeDtypeStruct((tiles, LANES), jnp.float32),
        in_specs=[pl.BlockSpec(memory_space=pltpu.SMEM)] + [vmem] * 7,
        out_specs=vmem,
        scratch_shapes=[
            pltpu.VMEM((WIN, LANES, M), jnp.bfloat16),
            pltpu.VMEM((8, LANES), jnp.float32),
            pltpu.VMEM((-(-(tiles + AFTER + 8) // 8) * 8, LANES), jnp.float32),
            pltpu.VMEM((bands, pad, LANES), jnp.float32),
            pltpu.VMEM((bands, pad, LANES), jnp.float32),
            pltpu.VMEM((bands, pad, LANES), jnp.float32),
            pltpu.VMEM((STEPS, bands * pad + 8, LANES), jnp.float32),
            pltpu.VMEM((bands, LANES, LANES), jnp.float32),
            pltpu.VMEM((bands, LANES, LANES), jnp.float32),
            pltpu.VMEM((bands, UNROLL // PHASES, M, LANES), jnp.bfloat16),
            pltpu.VMEM((bands, UNROLL // PHASES, M, LANES), jnp.bfloat16),
            pltpu.VMEM((bands, M, LANES), jnp.bfloat16),
            pltpu.VMEM((bands, M, LANES), jnp.bfloat16),
            pltpu.VMEM((tiles, LANES, LANES), jnp.float32),
        ],
        compiler_params=pltpu.CompilerParams(vmem_limit_bytes=VMEM_LIMIT),
    )(starts, own, halo, tail, main, side, factor, z)


def body(series, tail, band_starts):
    block_len = series.shape[0]
    rows = block_len // LANES
    devices, cores = lax.axis_size("tm"), lax.axis_size("band")
    distance = BAND_BASE // block_len
    tiles = rows // cores
    position, core = lax.axis_index("tm"), lax.axis_index("band")
    own = series.reshape(rows, LANES)
    tail = tail.reshape(WIN, LANES)

    def move(value, steps):
        route = [
            ((d + s) * cores + c, d * cores + c) for d, c, s in steps if 0 <= d + s < devices
        ]
        return lax.ppermute(value, ("tm", "band"), route)

    row_side = range(devices - distance)
    col_side = range(distance, devices)
    main_row = [(d, c, distance) for d in row_side for c in range(cores)]
    main_col = [(d, c, -distance) for d in col_side for c in range(cores)]
    side_row = [(d, 1, distance + 1) for d in row_side]
    side_col = [(d, 0, -distance - 1) for d in col_side] + [(d, 1, 1 - distance) for d in col_side]
    merged = devices <= 2 * distance
    roles = [(None, main_row + main_col, side_row + side_col)] if merged else [
        (False, main_row, side_row),
        (True, main_col, side_col),
    ]
    halo = move(own, [(d, 1, 1) for d in range(devices)])
    sides = [move(own, pairs) for _, _, pairs in roles]
    mains = [move(own, pairs) for _, pairs, _ in roles]
    in_hbm = [pltpu.with_memory_space_constraint(value, pltpu.HBM) for value in (band_starts, tail, own)]
    z, factor, own, tail, starts = own_side(tiles, *in_hbm)
    found = []
    for (role, _, _), main, side in zip(roles, mains, sides):
        part = profile((devices, distance, rows, tiles, role), starts, own, halo, tail, main, side, factor, z)
        other = lax.ppermute(part, "band", [(0, 1), (1, 0)])
        mine = jnp.arange(cores)[:, None, None] == core
        found.append(jnp.where(mine, part[None], other[None]).reshape(-1))
    row_best = jnp.where(position < devices - distance, found[0], -1.0)
    col_best = jnp.where(position >= distance, found[-1], -1.0)
    return row_best, col_best


UNROLL = 32
OWN_UNROLL = 64
PHASES = 16
REDUCE = 64
VMEM_LIMIT = 24 << 20


def solution(mesh):
    placed = (P(("groups", "tm")), P("groups"), P("groups"))
    return jax.shard_map(
        body,
        mesh=mesh,
        in_specs=placed,
        out_specs=(P(("groups", "tm")), P(("groups", "tm"))),
        check_vma=False,
    )
```
